32 devices in a mesh: seq: 4 (over y, x), chan: 8 (over z, core).
Axes of the slice: x: 2, y: 2, z: 4, core: 2. Of those that a mesh axis runs over, the one named last changes fastest.
Arguments:
- hidden: bfloat16 [4096, 1024], P('chan', 'seq'), may hold values from -70 to 70
- gate_in: bfloat16 [4096, 1024], P('chan', 'seq'), may hold values from -4 to 4
- gate_out: bfloat16 [4096, 1024], P('chan', 'seq'), may hold values from -4 to 4
- filters: float32 [4096, 1024], P('chan', 'seq'), may hold values from -0.1875 to 0.1875
- norm_gain: float32 [4096], P('chan'), may hold values from 0.1 to 1.9
- skip_weight: float32 [4096], P('chan'), may hold values from -4 to 4
Outputs:
- mixed: bfloat16 [4096, 1024], P('chan', 'seq')
The draws below stay inside these ranges and needn't reach their ends.
All inputs are finite; a program needn't handle non-finite values.
Results may differ from the reference program's by a relative error of at most 0.0025.
Values sent between devices are 32-bit elements; how exact they have to be, the bound alone decides.
A program may use at most 64 MiB of HBM per device.

```python
import math
import jax
import jax.numpy as jnp
from jax import lax

CHANNELS = 4096
SEQ = 1024


def draw_hidden(key, part):
    first, second = jax.random.split(key)
    place = jnp.arange(CHANNELS, dtype=jnp.float32) / (CHANNELS - 1)
    rising = jnp.sqrt(1.0 + 2.0 * place)
    base = jax.random.truncated_normal(first, -4.0, 4.0, (CHANNELS, SEQ), jnp.float32)
    spread = jnp.exp(jax.random.uniform(second, (CHANNELS,), jnp.float32, 0.0, math.log(10.0)))
    return (base * (spread * rising)[:, None]).astype(jnp.bfloat16)


def block_levels(stream_key, extent, cuts, low, top_value):
    def one(dim, parts):
        draws = jax.random.uniform(jax.random.fold_in(jax.random.fold_in(stream_key, 6), dim), (parts,), jnp.float32, low / len(cuts), top_value / len(cuts))
        return jnp.repeat(jnp.exp(draws), extent[dim] // parts).reshape((-1,) + (1,) * (len(extent) - dim - 1))

    loudness = one(*cuts[0])
    for cut in cuts[1:]:
        loudness = loudness * one(*cut)
    return loudness


def noise(own_key, shape, scale, bound, cuts=(), kind=jnp.bfloat16):
    result = jax.random.normal(own_key, shape, jnp.float32) * scale
    if len(cuts) > 0:
        result = block_levels(own_key, shape, cuts, -0.22, 0.18) * result
    return jnp.clip(result, min=-bound, max=bound).astype(kind)


def setup_inputs(seed: int = 0) -> dict:
    key_of = jax.random.split(jax.random.key(seed), 7)
    return {
        "hidden": draw_hidden(jax.random.fold_in(key_of[6], 71), 0),
        "gate_in": noise(key_of[1], (CHANNELS, SEQ), 1.0, 4.0, ((0, 8), (1, 4))),
        "gate_out": noise(key_of[2], (CHANNELS, SEQ), 1.0, 4.0, ((0, 8), (1, 4))),
        "filters": noise(key_of[3], (CHANNELS, SEQ), SEQ ** -0.5, 0.1875, ((0, 8), (1, 4)), jnp.float32),
        "norm_gain": jnp.clip(1.0 + 0.18 * jax.random.normal(key_of[4], (CHANNELS,), jnp.float32), 0.1, 1.9),
        "skip_weight": noise(key_of[5], (CHANNELS,), 1.0, 4.0, ((0, 8),), jnp.float32),
    }


def reference(hidden, gate_in, gate_out, filters, norm_gain, skip_weight):
    activity = hidden.astype(jnp.float32)
    mean_sq = lax.optimization_barrier(jnp.sum(activity * activity, axis=0)) / CHANNELS + 1e-06
    normed = activity * lax.rsqrt(mean_sq)[None, :] * norm_gain[:, None]
    signal = gate_in.astype(jnp.float32) * normed
    fft_length = 2 * SEQ
    block = min(256, CHANNELS)

    def convolve(pair):
        signal_block, filter_block = pair
        spectrum = jnp.fft.rfft(signal_block, n=fft_length, axis=1) * jnp.fft.rfft(filter_block, n=fft_length, axis=1)
        return jnp.fft.irfft(spectrum, n=fft_length, axis=1)[:, :SEQ].astype(signal_block.dtype)
    blocks = (signal.reshape(CHANNELS // block, block, SEQ), filters.reshape(CHANNELS // block, block, SEQ))
    conv = lax.map(convolve, blocks).reshape(CHANNELS, SEQ)
    mixed = gate_out.astype(jnp.float32) * (conv + skip_weight[:, None] * signal)
    return mixed.astype(jnp.bfloat16)
```

```python
import functools
import math

import jax
import jax.numpy as jnp
import numpy as np
from jax import lax
from jax.experimental import pallas as pl
from jax.experimental.pallas import tpu as pltpu
from jax.sharding import PartitionSpec as P

highest = lax.Precision.HIGHEST
epsilon = 1e-06


def angle_table(row_count, col_count, period, sign):
    row_index = lax.iota(jnp.int32, row_count)[:, None]
    col_index = lax.iota(jnp.int32, col_count)[None, :]
    phase = (row_index * col_index % period).astype(jnp.float32) * (2.0 * math.pi / period)
    return (jnp.cos(phase), sign * jnp.sin(phase))


def twiddle_table(row_count, col_count, span, offset, period, sign):
    row_index = lax.iota(jnp.int32, row_count)[:, None]
    col_index = (lax.iota(jnp.int32, col_count) % span + offset)[None, :]
    phase = (row_index * col_index % period).astype(jnp.float32) * (2.0 * math.pi / period)
    return (jnp.cos(phase), sign * jnp.sin(phase))


def rotate(left_real, left_imag, right_real, right_imag):
    return (
        left_real * right_real - left_imag * right_imag,
        left_real * right_imag + left_imag * right_real,
    )


def sequence_forward(block, groups, span, offset, period):
    rows = 2 * groups
    cosine, sine = angle_table(rows, groups, rows, -1.0)
    both = jnp.dot(jnp.concatenate([cosine, sine], axis=0), block, precision=highest)
    real_part, imag_part = (both[:rows], both[rows:])
    turn_real, turn_imag = twiddle_table(rows, block.shape[1], span, offset, period, -1.0)
    return rotate(real_part, imag_part, turn_real, turn_imag)


def sequence_inverse(real_part, imag_part, groups, span, offset, period):
    rows = 2 * groups
    turn_real, turn_imag = twiddle_table(rows, real_part.shape[1], span, offset, period, 1.0)
    real_part, imag_part = rotate(real_part, imag_part, turn_real, turn_imag)
    cosine, sine = angle_table(groups, rows, rows, 1.0)
    return jnp.dot(cosine, real_part, precision=highest) - jnp.dot(
        sine, imag_part, precision=highest
    )


def full_transform(stacked, sign):
    length = stacked.shape[1]
    cosine, sine = angle_table(length, length, length, sign)
    return jnp.dot(stacked, jnp.concatenate([cosine, sine], axis=1), precision=highest)


def spectral_product(signal_real, signal_imag, filter_real, filter_imag):
    count, length = signal_real.shape
    stacked = jnp.concatenate([signal_real, signal_imag, filter_real, filter_imag], axis=0)
    spectra = full_transform(stacked, -1.0)
    s_real = spectra[:count, :length] - spectra[count : 2 * count, length:]
    s_imag = spectra[:count, length:] + spectra[count : 2 * count, :length]
    f_real = spectra[2 * count : 3 * count, :length] - spectra[3 * count :, length:]
    f_imag = spectra[2 * count : 3 * count, length:] + spectra[3 * count :, :length]
    product_real, product_imag = rotate(s_real, s_imag, f_real, f_imag)
    back = full_transform(jnp.concatenate([product_real, product_imag], axis=0), 1.0)
    return (
        back[:count, :length] - back[count:, length:],
        back[:count, length:] + back[count:, :length],
    )


def four_step(signal, filters, groups, width, period):
    channels, positions = signal.shape
    spread_signal, spread_filter = (
        lax.all_to_all(signal, "seq", split_axis=1, concat_axis=0, tiled=True),
        lax.all_to_all(filters, "seq", split_axis=1, concat_axis=0, tiled=True),
    )
    flat = (groups, channels * width)
    offset = lax.axis_index("seq") * width
    signal_real, signal_imag = sequence_forward(
        spread_signal.reshape(flat), groups, width, offset, period
    )
    filter_real, filter_imag = sequence_forward(
        spread_filter.reshape(flat), groups, width, offset, period
    )
    middle = (2 * groups, channels, width)
    signal_real, signal_imag, filter_real, filter_imag = (
        lax.all_to_all(signal_real.reshape(middle), "seq", split_axis=0, concat_axis=2, tiled=True),
        lax.all_to_all(signal_imag.reshape(middle), "seq", split_axis=0, concat_axis=2, tiled=True),
        lax.all_to_all(filter_real.reshape(middle), "seq", split_axis=0, concat_axis=2, tiled=True),
        lax.all_to_all(filter_imag.reshape(middle), "seq", split_axis=0, concat_axis=2, tiled=True),
    )
    rows = (2 * channels, positions)
    back_real, back_imag = spectral_product(
        signal_real.reshape(rows),
        signal_imag.reshape(rows),
        filter_real.reshape(rows),
        filter_imag.reshape(rows),
    )
    split = (2, channels, positions)
    back_real, back_imag = (
        lax.all_to_all(back_real.reshape(split), "seq", split_axis=2, concat_axis=0, tiled=True),
        lax.all_to_all(back_imag.reshape(split), "seq", split_axis=2, concat_axis=0, tiled=True),
    )
    wide = (2 * groups, channels * width)
    field = sequence_inverse(
        back_real.reshape(wide), back_imag.reshape(wide), groups, width, offset, period
    )
    result = lax.all_to_all(
        field.reshape(groups, channels, width), "seq", split_axis=0, concat_axis=2, tiled=True
    )
    return result.reshape(channels, positions) / period


def split_table(table):
    high = table.astype(jnp.bfloat16)
    low = (table - high.astype(np.float64)).astype(jnp.bfloat16)
    return high, low


def transform_tables(length, chunk, blocks):
    place = np.arange(length)[:, None]
    odd = 2 * np.arange(length)[None, :] + 1
    phase = (place * odd % (4 * length)) * (2.0 * np.pi / (4 * length))
    chunks = length // chunk
    cosine = np.cos(phase).reshape(length, chunks, chunk)
    sine = np.sin(phase).reshape(length, chunks, chunk)
    both = np.concatenate([cosine, -sine], axis=2)
    forward = both.transpose(1, 0, 2)
    inverse = both.reshape(length, 2 * length).T / length
    inverse = inverse.reshape(2 * length, blocks, length // blocks).transpose(1, 0, 2)
    return split_table(forward) + split_table(inverse)


def halves(value):
    high = value.astype(jnp.bfloat16)
    return high, (value - high.astype(jnp.float32)).astype(jnp.bfloat16)


def column(row, count, width):
    square = jnp.transpose(jnp.broadcast_to(row, (128, count)))
    return jnp.concatenate([square] * (width // 128), axis=1)


def conv_kernel(
    groups, peers, hidden, gate_in, gate_out, filters, gain, skip, fwd_hi, fwd_lo, inv_hi, inv_lo,
    mixed,
    fh, fl, ih, il, filter_in, signal_in, conv_in, conv_out, signal, local_sum, sums, halved, spectrum, product,
    table_sem, own_sem, f_send, f_recv, s_send, s_recv, c_send, c_recv, q_send, q_recv,
):
    me = lax.axis_index("seq")
    row = lax.axis_index("chan")
    count = hidden.shape[0] // groups
    width = hidden.shape[1]

    barrier = pltpu.get_barrier_semaphore()
    for step in range(1, groups):
        pl.semaphore_signal(
            barrier, inc=1, device_id={"seq": lax.rem(me + step, groups)}, device_id_type=pl.DeviceIdType.MESH
        )
    for step in range(1, peers):
        pl.semaphore_signal(
            barrier, inc=1, device_id={"chan": lax.rem(row + step, peers)}, device_id_type=pl.DeviceIdType.MESH
        )
    pl.semaphore_wait(barrier, groups + peers - 2)

    def send(step, source, target, sent, received):
        to = lax.rem(me + step, groups)
        copy = pltpu.make_async_remote_copy(
            src_ref=source.at[to], dst_ref=target.at[me], send_sem=sent.at[step], recv_sem=received.at[step],
            device_id={"seq": to}, device_id_type=pl.DeviceIdType.MESH,
        )
        copy.start()
        return copy

    order = [groups // 2] + [s for s in range(1, groups) if s != groups // 2]
    filter_copies = []
    for step in range(1, groups):
        to = lax.rem(me + step, groups)
        copy = pltpu.make_async_remote_copy(
            src_ref=filters.at[pl.ds(to * count, count), :], dst_ref=filter_in.at[me],
            send_sem=f_send.at[step], recv_sem=f_recv.at[step],
            device_id={"seq": to}, device_id_type=pl.DeviceIdType.MESH,
        )
        copy.start()
        filter_copies.append(copy)
    own_filter = pltpu.make_async_copy(filters.at[pl.ds(me * count, count), :], filter_in.at[me], own_sem.at[0])
    own_filter.start()
    tables = []
    for index, (source, target) in enumerate(((fwd_hi, fh), (fwd_lo, fl), (inv_hi, ih), (inv_lo, il))):
        copy = pltpu.make_async_copy(source, target, table_sem.at[index])
        copy.start()
        tables.append(copy)

    partial = jnp.zeros((1, width), jnp.float32)
    for block in range(groups):
        activity = hidden[block * count : (block + 1) * count, :].astype(jnp.float32)
        partial = partial + jnp.sum(activity * activity, axis=0, keepdims=True)
    local_sum[...] = partial
    sums[row] = partial
    sum_copies = []
    for step in range(1, peers):
        copy = pltpu.make_async_remote_copy(
            src_ref=local_sum, dst_ref=sums.at[row], send_sem=q_send.at[step], recv_sem=q_recv.at[step],
            device_id={"chan": lax.rem(row + step, peers)}, device_id_type=pl.DeviceIdType.MESH,
        )
        copy.start()
        sum_copies.append(copy)
    for copy in sum_copies:
        copy.wait()
    total = sums[0]
    for index in range(1, peers):
        total = total + sums[index]
    scale = lax.rsqrt(total / (hidden.shape[0] * peers) + epsilon)
    for block in range(groups):
        rows = slice(block * count, (block + 1) * count)
        normed = hidden[rows, :].astype(jnp.float32) * scale * column(gain[:, rows], count, width)
        signal[block] = gate_in[rows, :].astype(jnp.float32) * normed
    signal_copies = [send(step, signal, signal_in, s_send, s_recv) for step in range(1, groups)]
    own_signal = pltpu.make_async_copy(signal.at[me], signal_in.at[me], own_sem.at[1])
    own_signal.start()

    def load_halves(source):
        for block in range(groups):
            high, low = halves(source[block])
            halved[:count, block * width : (block + 1) * width] = high
            halved[count:, block * width : (block + 1) * width] = low

    def transform(index):
        both = jnp.dot(halved[...], fh[index], preferred_element_type=jnp.float32)
        small = jnp.dot(halved[:count, :], fl[index], preferred_element_type=jnp.float32)
        return both[:count] + (both[count:] + small)

    chunks = fh.shape[0]
    chunk = fh.shape[2] // 2
    for copy in filter_copies:
        copy.wait()
    own_filter.wait()
    load_halves(filter_in)
    tables[0].wait()
    tables[1].wait()

    def filter_step(index, carry):
        spectrum[index] = transform(index)
        return carry

    lax.fori_loop(0, chunks, filter_step, 0)
    for copy in signal_copies:
        copy.wait()
    own_signal.wait()
    load_halves(signal_in)

    for index in range(chunks):
        s_both = transform(index)
        s_real, s_imag = s_both[:, :chunk], s_both[:, chunk:]
        f_both = spectrum[index]
        f_real, f_imag = f_both[:, :chunk], f_both[:, chunk:]
        real_high, real_low = halves(s_real * f_real - s_imag * f_imag)
        imag_high, imag_low = halves(s_real * f_imag + s_imag * f_real)
        start = 2 * index * chunk
        product[:count, start : start + chunk] = real_high
        product[count:, start : start + chunk] = real_low
        product[:count, start + chunk : start + 2 * chunk] = imag_high
        product[count:, start + chunk : start + 2 * chunk] = imag_low

    tables[2].wait()
    tables[3].wait()

    def invert(block):
        both = jnp.dot(product[...], ih[block], preferred_element_type=jnp.float32)
        small = jnp.dot(product[:count, :], il[block], preferred_element_type=jnp.float32)
        return both[:count] + (both[count:] + small)

    conv_copies = []
    for step in order:
        to = lax.rem(me + step, groups)
        conv_out[to] = invert(to)
        conv_copies.append(send(step, conv_out, conv_in, c_send, c_recv))
    conv_in[me] = invert(me)
    for copy in conv_copies:
        copy.wait()
    for block in range(groups):
        rows = slice(block * count, (block + 1) * count)
        direct = column(skip[:, rows], count, width) * signal[block]
        mixed[rows, :] = (gate_out[rows, :].astype(jnp.float32) * (conv_in[block] + direct)).astype(jnp.bfloat16)


def fused(hidden, gate_in, gate_out, filters, norm_gain, skip_weight):
    channels, width = hidden.shape
    groups, peers = lax.axis_size("seq"), lax.axis_size("chan")
    length, count = groups * width, channels // groups
    chunk = min(256, length)
    tables = [jnp.asarray(t) for t in transform_tables(length, chunk, groups)]
    vmem = pl.BlockSpec(memory_space=pltpu.VMEM)
    hbm = pl.BlockSpec(memory_space=pl.ANY)
    block = (groups, count, width)
    f32, bf16 = jnp.float32, jnp.bfloat16
    pair = pltpu.SemaphoreType.DMA((groups,))
    ring = pltpu.SemaphoreType.DMA((peers,))
    return pl.pallas_call(
        functools.partial(conv_kernel, groups, peers),
        out_shape=jax.ShapeDtypeStruct((channels, width), bf16),
        in_specs=[vmem, vmem, vmem, hbm, vmem, vmem, hbm, hbm, hbm, hbm],
        out_specs=vmem,
        scratch_shapes=[
            pltpu.VMEM(tables[0].shape, bf16),
            pltpu.VMEM(tables[1].shape, bf16),
            pltpu.VMEM(tables[2].shape, bf16),
            pltpu.VMEM(tables[3].shape, bf16),
            pltpu.VMEM(block, f32),
            pltpu.VMEM(block, f32),
            pltpu.VMEM(block, f32),
            pltpu.VMEM(block, f32),
            pltpu.VMEM(block, f32),
            pltpu.VMEM((1, width), f32),
            pltpu.VMEM((peers, 1, width), f32),
            pltpu.VMEM((2 * count, length), bf16),
            pltpu.VMEM((length // chunk, count, 2 * chunk), f32),
            pltpu.VMEM((2 * count, 2 * length), bf16),
            pltpu.SemaphoreType.DMA((4,)),
            pltpu.SemaphoreType.DMA((2,)),
            pair, pair, pair, pair, pair, pair, ring, ring,
        ],
        compiler_params=pltpu.CompilerParams(
            collective_id=0, has_side_effects=True, vmem_limit_bytes=56 * 1024 * 1024
        ),
    )(hidden, gate_in, gate_out, filters, norm_gain.reshape(1, channels), skip_weight.reshape(1, channels), *tables)


def per_device(hidden, gate_in, gate_out, filters, norm_gain, skip_weight):
    length = hidden.shape[1] * lax.axis_size("seq")
    if 16 * length * length <= 2**24 and hidden.shape[0] == 128 * lax.axis_size("seq"):
        return fused(hidden, gate_in, gate_out, filters, norm_gain, skip_weight)
    activity = hidden.astype(jnp.float32)
    channels, positions = activity.shape
    squares = lax.psum(jnp.sum(activity * activity, axis=0), "chan")
    mean_sq = squares / (channels * lax.axis_size("chan")) + epsilon
    normed = activity * lax.rsqrt(mean_sq)[None, :] * norm_gain[:, None]
    signal = gate_in.astype(jnp.float32) * normed
    groups = lax.axis_size("seq")
    width = positions // groups
    period = 2 * positions * groups
    conv = four_step(signal, filters, groups, width, period)
    mixed = gate_out.astype(jnp.float32) * (conv + skip_weight[:, None] * signal)
    return mixed.astype(jnp.bfloat16)


def solution(mesh):
    placed = (
        P("chan", "seq"),
        P("chan", "seq"),
        P("chan", "seq"),
        P("chan", "seq"),
        P("chan"),
        P("chan"),
    )
    return jax.shard_map(
        per_device, mesh=mesh, in_specs=placed, out_specs=P("chan", "seq"), check_vma=False
    )
```

```python
import functools
import math

import jax
import jax.numpy as jnp
import numpy as np
from jax import lax
from jax.experimental import pallas as pl
from jax.experimental.pallas import tpu as pltpu
from jax.sharding import PartitionSpec as P

highest = lax.Precision.HIGHEST
epsilon = 1e-06


def angle_table(row_count, col_count, period, sign):
    row_index = lax.iota(jnp.int32, row_count)[:, None]
    col_index = lax.iota(jnp.int32, col_count)[None, :]
    phase = (row_index * col_index % period).astype(jnp.float32) * (2.0 * math.pi / period)
    return (jnp.cos(phase), sign * jnp.sin(phase))


def twiddle_table(row_count, col_count, span, offset, period, sign):
    row_index = lax.iota(jnp.int32, row_count)[:, None]
    col_index = (lax.iota(jnp.int32, col_count) % span + offset)[None, :]
    phase = (row_index * col_index % period).astype(jnp.float32) * (2.0 * math.pi / period)
    return (jnp.cos(phase), sign * jnp.sin(phase))


def rotate(left_real, left_imag, right_real, right_imag):
    return (
        left_real * right_real - left_imag * right_imag,
        left_real * right_imag + left_imag * right_real,
    )


def sequence_forward(block, groups, span, offset, period):
    rows = 2 * groups
    cosine, sine = angle_table(rows, groups, rows, -1.0)
    both = jnp.dot(jnp.concatenate([cosine, sine], axis=0), block, precision=highest)
    real_part, imag_part = (both[:rows], both[rows:])
    turn_real, turn_imag = twiddle_table(rows, block.shape[1], span, offset, period, -1.0)
    return rotate(real_part, imag_part, turn_real, turn_imag)


def sequence_inverse(real_part, imag_part, groups, span, offset, period):
    rows = 2 * groups
    turn_real, turn_imag = twiddle_table(rows, real_part.shape[1], span, offset, period, 1.0)
    real_part, imag_part = rotate(real_part, imag_part, turn_real, turn_imag)
    cosine, sine = angle_table(groups, rows, rows, 1.0)
    return jnp.dot(cosine, real_part, precision=highest) - jnp.dot(
        sine, imag_part, precision=highest
    )


def full_transform(stacked, sign):
    length = stacked.shape[1]
    cosine, sine = angle_table(length, length, length, sign)
    return jnp.dot(stacked, jnp.concatenate([cosine, sine], axis=1), precision=highest)


def spectral_product(signal_real, signal_imag, filter_real, filter_imag):
    count, length = signal_real.shape
    stacked = jnp.concatenate([signal_real, signal_imag, filter_real, filter_imag], axis=0)
    spectra = full_transform(stacked, -1.0)
    s_real = spectra[:count, :length] - spectra[count : 2 * count, length:]
    s_imag = spectra[:count, length:] + spectra[count : 2 * count, :length]
    f_real = spectra[2 * count : 3 * count, :length] - spectra[3 * count :, length:]
    f_imag = spectra[2 * count : 3 * count, length:] + spectra[3 * count :, :length]
    product_real, product_imag = rotate(s_real, s_imag, f_real, f_imag)
    back = full_transform(jnp.concatenate([product_real, product_imag], axis=0), 1.0)
    return (
        back[:count, :length] - back[count:, length:],
        back[:count, length:] + back[count:, :length],
    )


def four_step(signal, filters, groups, width, period):
    channels, positions = signal.shape
    spread_signal, spread_filter = (
        lax.all_to_all(signal, "seq", split_axis=1, concat_axis=0, tiled=True),
        lax.all_to_all(filters, "seq", split_axis=1, concat_axis=0, tiled=True),
    )
    flat = (groups, channels * width)
    offset = lax.axis_index("seq") * width
    signal_real, signal_imag = sequence_forward(
        spread_signal.reshape(flat), groups, width, offset, period
    )
    filter_real, filter_imag = sequence_forward(
        spread_filter.reshape(flat), groups, width, offset, period
    )
    middle = (2 * groups, channels, width)
    signal_real, signal_imag, filter_real, filter_imag = (
        lax.all_to_all(signal_real.reshape(middle), "seq", split_axis=0, concat_axis=2, tiled=True),
        lax.all_to_all(signal_imag.reshape(middle), "seq", split_axis=0, concat_axis=2, tiled=True),
        lax.all_to_all(filter_real.reshape(middle), "seq", split_axis=0, concat_axis=2, tiled=True),
        lax.all_to_all(filter_imag.reshape(middle), "seq", split_axis=0, concat_axis=2, tiled=True),
    )
    rows = (2 * channels, positions)
    back_real, back_imag = spectral_product(
        signal_real.reshape(rows),
        signal_imag.reshape(rows),
        filter_real.reshape(rows),
        filter_imag.reshape(rows),
    )
    split = (2, channels, positions)
    back_real, back_imag = (
        lax.all_to_all(back_real.reshape(split), "seq", split_axis=2, concat_axis=0, tiled=True),
        lax.all_to_all(back_imag.reshape(split), "seq", split_axis=2, concat_axis=0, tiled=True),
    )
    wide = (2 * groups, channels * width)
    field = sequence_inverse(
        back_real.reshape(wide), back_imag.reshape(wide), groups, width, offset, period
    )
    result = lax.all_to_all(
        field.reshape(groups, channels, width), "seq", split_axis=0, concat_axis=2, tiled=True
    )
    return result.reshape(channels, positions) / period


def split_table(table):
    high = table.astype(jnp.bfloat16)
    low = (table - high.astype(np.float64)).astype(jnp.bfloat16)
    return high, low


def transform_tables(length, chunk, blocks):
    place = np.arange(length)[:, None]
    odd = 2 * np.arange(length)[None, :] + 1
    phase = (place * odd % (4 * length)) * (2.0 * np.pi / (4 * length))
    chunks = length // chunk
    cosine = np.cos(phase).reshape(length, chunks, chunk)
    sine = np.sin(phase).reshape(length, chunks, chunk)
    both = np.concatenate([cosine, -sine], axis=2)
    forward = both.transpose(1, 0, 2)
    inverse = both.reshape(length, 2 * length).T / length
    inverse = inverse.reshape(2 * length, blocks, length // blocks).transpose(1, 0, 2)
    return split_table(forward) + split_table(inverse)


def halves(value):
    high = value.astype(jnp.bfloat16)
    return high, (value - high.astype(jnp.float32)).astype(jnp.bfloat16)


def column(row, count, width):
    square = jnp.transpose(jnp.broadcast_to(row, (128, count)))
    return jnp.concatenate([square] * (width // 128), axis=1)


def conv_kernel(
    groups, peers, hidden_hbm, gate_hbm, filters, gain, fwd_hi, fwd_lo, inv_hi, inv_lo,
    conv_in, scale_out,
    fh, fl, ih, il, hidden, gate_in, filter_in, signal_in, conv_out, signal, local_sum, sums, scales, halved, spectrum,
    product,
    table_sem, own_sem, f_send, f_recv, s_send, s_recv, c_send, c_recv, r_send, r_recv, q_send, q_recv,
):
    me = lax.axis_index("seq")
    row = lax.axis_index("chan")
    count = hidden.shape[0] // groups
    width = hidden.shape[1]

    def local(source, target, sem):
        copy = pltpu.make_async_copy(source, target, sem)
        copy.start()
        return copy

    def rows_of(block):
        return pl.ds(pl.multiple_of(block * count, count), count)

    def send(step, source, target, sent, received):
        copy = pltpu.make_async_remote_copy(
            src_ref=source, dst_ref=target, send_sem=sent.at[step], recv_sem=received.at[step],
            device_id={"seq": lax.rem(me + step, groups)}, device_id_type=pl.DeviceIdType.MESH,
        )
        copy.start()
        return copy

    barrier = pltpu.get_barrier_semaphore()
    for step in range(1, groups):
        pl.semaphore_signal(
            barrier, inc=1, device_id={"seq": lax.rem(me + step, groups)}, device_id_type=pl.DeviceIdType.MESH
        )
    for step in range(1, peers):
        pl.semaphore_signal(
            barrier, inc=1, device_id={"chan": lax.rem(row + step, peers)}, device_id_type=pl.DeviceIdType.MESH
        )
    own_hidden = local(hidden_hbm, hidden, own_sem.at[1])
    own_gate = local(gate_hbm, gate_in, own_sem.at[2])
    own_filter = local(filters.at[rows_of(me), :], filter_in.at[me], own_sem.at[0])
    tables = [
        local(source, target, table_sem.at[index])
        for index, (source, target) in enumerate(((fwd_hi, fh), (fwd_lo, fl), (inv_hi, ih), (inv_lo, il)))
    ]
    own_hidden.wait()
    partial = jnp.zeros((1, width), jnp.float32)
    for block in range(groups):
        activity = hidden[block * count : (block + 1) * count, :].astype(jnp.float32)
        partial = partial + jnp.sum(activity * activity, axis=0, keepdims=True)
    local_sum[...] = partial
    sums[row] = partial
    pl.semaphore_wait(barrier, groups + peers - 2)

    order = [groups // 2] + [s for s in range(1, groups) if s != groups // 2]
    filter_copies = [
        send(step, filters.at[rows_of(lax.rem(me + step, groups)), :], filter_in.at[me], f_send, f_recv)
        for step in range(1, groups)
    ]
    sum_copies = []
    for step in range(1, peers):
        copy = pltpu.make_async_remote_copy(
            src_ref=local_sum, dst_ref=sums.at[row], send_sem=q_send.at[step], recv_sem=q_recv.at[step],
            device_id={"chan": lax.rem(row + step, peers)}, device_id_type=pl.DeviceIdType.MESH,
        )
        copy.start()
        sum_copies.append(copy)

    def gated(block):
        rows = rows_of(block)
        scaled = hidden[rows, :].astype(jnp.float32) * column(gain[block], count, width)
        return gate_in[rows, :].astype(jnp.float32) * scaled

    own_gate.wait()
    signal_copies = []
    for step in range(1, groups):
        to = lax.rem(me + step, groups)
        signal[to] = gated(to)
        signal_copies.append(send(step, signal.at[to], signal_in.at[me], s_send, s_recv))
    signal_in[me] = gated(me)

    for copy in sum_copies:
        copy.wait()
    total = sums[0]
    for index in range(1, peers):
        total = total + sums[index]
    scale = lax.rsqrt(total / (hidden.shape[0] * peers) + epsilon)
    scale_out[...] = scale
    scales[me] = scale
    scale_copies = [send(step, scales.at[me], scales.at[me], r_send, r_recv) for step in range(1, groups)]

    def store_halves(block, value):
        high, low = halves(value)
        halved[:count, block * width : (block + 1) * width] = high
        halved[count:, block * width : (block + 1) * width] = low

    def transform(index):
        both = jnp.dot(halved[...], fh[index], preferred_element_type=jnp.float32)
        small = jnp.dot(halved[:count, :], fl[index], preferred_element_type=jnp.float32)
        return both[:count] + (both[count:] + small)

    chunks = fh.shape[0]
    chunk = fh.shape[2] // 2
    for copy in filter_copies:
        copy.wait()
    own_filter.wait()
    for block in range(groups):
        store_halves(block, filter_in[block])
    tables[0].wait()
    tables[1].wait()

    def filter_step(index, carry):
        spectrum[index] = transform(index)
        return carry

    lax.fori_loop(0, chunks, filter_step, 0)
    for copy in signal_copies + scale_copies:
        copy.wait()
    for block in range(groups):
        store_halves(block, signal_in[block] * scales[block])

    for index in range(chunks):
        s_both = transform(index)
        s_real, s_imag = s_both[:, :chunk], s_both[:, chunk:]
        f_both = spectrum[index]
        f_real, f_imag = f_both[:, :chunk], f_both[:, chunk:]
        real_high, real_low = halves(s_real * f_real - s_imag * f_imag)
        imag_high, imag_low = halves(s_real * f_imag + s_imag * f_real)
        start = 2 * index * chunk
        product[:count, start : start + chunk] = real_high
        product[count:, start : start + chunk] = real_low
        product[:count, start + chunk : start + 2 * chunk] = imag_high
        product[count:, start + chunk : start + 2 * chunk] = imag_low

    tables[2].wait()
    tables[3].wait()

    def invert(block):
        both = jnp.dot(product[...], ih[block], preferred_element_type=jnp.float32)
        small = jnp.dot(product[:count, :], il[block], preferred_element_type=jnp.float32)
        return both[:count] + (both[count:] + small)

    conv_copies = []
    for step in order:
        to = lax.rem(me + step, groups)
        conv_out[to] = invert(to)
        conv_copies.append(send(step, conv_out.at[to], conv_in.at[me], c_send, c_recv))
    conv_out[me] = invert(me)
    own_conv = local(conv_out.at[me], conv_in.at[me], own_sem.at[3])
    for copy in conv_copies:
        copy.wait()
    own_conv.wait()


def fused(hidden, gate_in, gate_out, filters, norm_gain, skip_weight):
    channels, width = hidden.shape
    groups, peers = lax.axis_size("seq"), lax.axis_size("chan")
    length, count = groups * width, channels // groups
    chunk = min(256, length)
    tables = [jnp.asarray(t) for t in transform_tables(length, chunk, groups)]
    vmem = pl.BlockSpec(memory_space=pltpu.VMEM)
    hbm = pl.BlockSpec(memory_space=pl.ANY)
    block = (groups, count, width)
    f32, bf16 = jnp.float32, jnp.bfloat16
    pair = pltpu.SemaphoreType.DMA((groups,))
    ring = pltpu.SemaphoreType.DMA((peers,))
    conv, scale = pl.pallas_call(
        functools.partial(conv_kernel, groups, peers),
        out_shape=[jax.ShapeDtypeStruct(block, f32), jax.ShapeDtypeStruct((1, width), f32)],
        in_specs=[hbm, hbm, hbm, vmem, hbm, hbm, hbm, hbm],
        out_specs=[hbm, vmem],
        scratch_shapes=[
            pltpu.VMEM(tables[0].shape, bf16),
            pltpu.VMEM(tables[1].shape, bf16),
            pltpu.VMEM(tables[2].shape, bf16),
            pltpu.VMEM(tables[3].shape, bf16),
            pltpu.VMEM((channels, width), bf16),
            pltpu.VMEM((channels, width), bf16),
            pltpu.VMEM(block, f32),
            pltpu.VMEM(block, f32),
            pltpu.VMEM(block, f32),
            pltpu.VMEM(block, f32),
            pltpu.VMEM((1, width), f32),
            pltpu.VMEM((peers, 1, width), f32),
            pltpu.VMEM((groups, 1, width), f32),
            pltpu.VMEM((2 * count, length), bf16),
            pltpu.VMEM((length // chunk, count, 2 * chunk), f32),
            pltpu.VMEM((2 * count, 2 * length), bf16),
            pltpu.SemaphoreType.DMA((4,)),
            pltpu.SemaphoreType.DMA((4,)),
            pair, pair, pair, pair, pair, pair, pair, pair, ring, ring,
        ],
        compiler_params=pltpu.CompilerParams(
            collective_id=0, has_side_effects=True, vmem_limit_bytes=56 * 1024 * 1024
        ),
    )(hidden, gate_in, filters, norm_gain.reshape(groups, 1, count), *tables)
    signal = gate_in.astype(f32) * (hidden.astype(f32) * norm_gain[:, None]) * scale
    mixed = gate_out.astype(f32) * (conv.reshape(channels, width) + skip_weight[:, None] * signal)
    return mixed.astype(bf16)


def per_device(hidden, gate_in, gate_out, filters, norm_gain, skip_weight):
    length = hidden.shape[1] * lax.axis_size("seq")
    if 16 * length * length <= 2**24 and hidden.shape[0] == 128 * lax.axis_size("seq"):
        return fused(hidden, gate_in, gate_out, filters, norm_gain, skip_weight)
    activity = hidden.astype(jnp.float32)
    channels, positions = activity.shape
    squares = lax.psum(jnp.sum(activity * activity, axis=0), "chan")
    mean_sq = squares / (channels * lax.axis_size("chan")) + epsilon
    normed = activity * lax.rsqrt(mean_sq)[None, :] * norm_gain[:, None]
    signal = gate_in.astype(jnp.float32) * normed
    groups = lax.axis_size("seq")
    width = positions // groups
    period = 2 * positions * groups
    conv = four_step(signal, filters, groups, width, period)
    mixed = gate_out.astype(jnp.float32) * (conv + skip_weight[:, None] * signal)
    return mixed.astype(jnp.bfloat16)


def solution(mesh):
    placed = (
        P("chan", "seq"),
        P("chan", "seq"),
        P("chan", "seq"),
        P("chan", "seq"),
        P("chan"),
        P("chan"),
    )
    return jax.shard_map(
        per_device, mesh=mesh, in_specs=placed, out_specs=P("chan", "seq"), check_vma=False
    )
```

```python
import functools
import math

import jax
import jax.numpy as jnp
import numpy as np
from jax import lax
from jax.experimental import pallas as pl
from jax.experimental.pallas import tpu as pltpu
from jax.sharding import PartitionSpec as P

highest = lax.Precision.HIGHEST
epsilon = 1e-06


def angle_table(row_count, col_count, period, sign):
    row_index = lax.iota(jnp.int32, row_count)[:, None]
    col_index = lax.iota(jnp.int32, col_count)[None, :]
    phase = (row_index * col_index % period).astype(jnp.float32) * (2.0 * math.pi / period)
    return (jnp.cos(phase), sign * jnp.sin(phase))


def twiddle_table(row_count, col_count, span, offset, period, sign):
    row_index = lax.iota(jnp.int32, row_count)[:, None]
    col_index = (lax.iota(jnp.int32, col_count) % span + offset)[None, :]
    phase = (row_index * col_index % period).astype(jnp.float32) * (2.0 * math.pi / period)
    return (jnp.cos(phase), sign * jnp.sin(phase))


def rotate(left_real, left_imag, right_real, right_imag):
    return (
        left_real * right_real - left_imag * right_imag,
        left_real * right_imag + left_imag * right_real,
    )


def sequence_forward(block, groups, span, offset, period):
    rows = 2 * groups
    cosine, sine = angle_table(rows, groups, rows, -1.0)
    both = jnp.dot(jnp.concatenate([cosine, sine], axis=0), block, precision=highest)
    real_part, imag_part = (both[:rows], both[rows:])
    turn_real, turn_imag = twiddle_table(rows, block.shape[1], span, offset, period, -1.0)
    return rotate(real_part, imag_part, turn_real, turn_imag)


def sequence_inverse(real_part, imag_part, groups, span, offset, period):
    rows = 2 * groups
    turn_real, turn_imag = twiddle_table(rows, real_part.shape[1], span, offset, period, 1.0)
    real_part, imag_part = rotate(real_part, imag_part, turn_real, turn_imag)
    cosine, sine = angle_table(groups, rows, rows, 1.0)
    return jnp.dot(cosine, real_part, precision=highest) - jnp.dot(
        sine, imag_part, precision=highest
    )


def full_transform(stacked, sign):
    length = stacked.shape[1]
    cosine, sine = angle_table(length, length, length, sign)
    return jnp.dot(stacked, jnp.concatenate([cosine, sine], axis=1), precision=highest)


def spectral_product(signal_real, signal_imag, filter_real, filter_imag):
    count, length = signal_real.shape
    stacked = jnp.concatenate([signal_real, signal_imag, filter_real, filter_imag], axis=0)
    spectra = full_transform(stacked, -1.0)
    s_real = spectra[:count, :length] - spectra[count : 2 * count, length:]
    s_imag = spectra[:count, length:] + spectra[count : 2 * count, :length]
    f_real = spectra[2 * count : 3 * count, :length] - spectra[3 * count :, length:]
    f_imag = spectra[2 * count : 3 * count, length:] + spectra[3 * count :, :length]
    product_real, product_imag = rotate(s_real, s_imag, f_real, f_imag)
    back = full_transform(jnp.concatenate([product_real, product_imag], axis=0), 1.0)
    return (
        back[:count, :length] - back[count:, length:],
        back[:count, length:] + back[count:, :length],
    )


def four_step(signal, filters, groups, width, period):
    channels, positions = signal.shape
    spread_signal, spread_filter = (
        lax.all_to_all(signal, "seq", split_axis=1, concat_axis=0, tiled=True),
        lax.all_to_all(filters, "seq", split_axis=1, concat_axis=0, tiled=True),
    )
    flat = (groups, channels * width)
    offset = lax.axis_index("seq") * width
    signal_real, signal_imag = sequence_forward(
        spread_signal.reshape(flat), groups, width, offset, period
    )
    filter_real, filter_imag = sequence_forward(
        spread_filter.reshape(flat), groups, width, offset, period
    )
    middle = (2 * groups, channels, width)
    signal_real, signal_imag, filter_real, filter_imag = (
        lax.all_to_all(signal_real.reshape(middle), "seq", split_axis=0, concat_axis=2, tiled=True),
        lax.all_to_all(signal_imag.reshape(middle), "seq", split_axis=0, concat_axis=2, tiled=True),
        lax.all_to_all(filter_real.reshape(middle), "seq", split_axis=0, concat_axis=2, tiled=True),
        lax.all_to_all(filter_imag.reshape(middle), "seq", split_axis=0, concat_axis=2, tiled=True),
    )
    rows = (2 * channels, positions)
    back_real, back_imag = spectral_product(
        signal_real.reshape(rows),
        signal_imag.reshape(rows),
        filter_real.reshape(rows),
        filter_imag.reshape(rows),
    )
    split = (2, channels, positions)
    back_real, back_imag = (
        lax.all_to_all(back_real.reshape(split), "seq", split_axis=2, concat_axis=0, tiled=True),
        lax.all_to_all(back_imag.reshape(split), "seq", split_axis=2, concat_axis=0, tiled=True),
    )
    wide = (2 * groups, channels * width)
    field = sequence_inverse(
        back_real.reshape(wide), back_imag.reshape(wide), groups, width, offset, period
    )
    result = lax.all_to_all(
        field.reshape(groups, channels, width), "seq", split_axis=0, concat_axis=2, tiled=True
    )
    return result.reshape(channels, positions) / period


def split_table(table):
    high = table.astype(jnp.bfloat16)
    low = (table - high.astype(np.float64)).astype(jnp.bfloat16)
    return high, low


def transform_tables(length, chunk, blocks):
    place = np.arange(length)[:, None]
    odd = 2 * np.arange(length)[None, :] + 1
    phase = (place * odd % (4 * length)) * (2.0 * np.pi / (4 * length))
    chunks = length // chunk
    cosine = np.cos(phase).reshape(length, chunks, chunk)
    sine = np.sin(phase).reshape(length, chunks, chunk)
    both = np.concatenate([cosine, -sine], axis=2)
    forward = both.transpose(1, 0, 2)
    inverse = both.reshape(length, 2 * length).T / length
    inverse = inverse.reshape(2 * length, blocks, length // blocks).transpose(1, 0, 2)
    return split_table(forward) + split_table(inverse)


def halves(value):
    high = value.astype(jnp.bfloat16)
    return high, (value - high.astype(jnp.float32)).astype(jnp.bfloat16)


def column(row, count, width):
    square = jnp.transpose(jnp.broadcast_to(row, (128, count)))
    return jnp.concatenate([square] * (width // 128), axis=1)


def conv_kernel(
    groups, peers, hidden_hbm, gate_hbm, filters, gain, fwd_hi, fwd_lo, inv_hi, inv_lo,
    conv_in, scale_out,
    fh, fl, ih, il, hidden, gate_in, filter_in, signal_in, conv_out, signal, local_sum, sums, scales, halved, spectrum,
    product,
    table_sem, own_sem, f_send, f_recv, s_send, s_recv, c_send, c_recv, r_send, r_recv, q_send, q_recv,
):
    me = lax.axis_index("seq")
    row = lax.axis_index("chan")
    count = hidden.shape[0] // groups
    width = hidden.shape[1]
    parts = filter_in.shape[0]
    sub = count // parts

    def local(source, target, sem):
        copy = pltpu.make_async_copy(source, target, sem)
        copy.start()
        return copy

    def send(slot, step, source, target, sent, received):
        copy = pltpu.make_async_remote_copy(
            src_ref=source, dst_ref=target, send_sem=sent.at[slot], recv_sem=received.at[slot],
            device_id={"seq": lax.rem(me + step, groups)}, device_id_type=pl.DeviceIdType.MESH,
        )
        copy.start()
        return copy

    barrier = pltpu.get_barrier_semaphore()
    for step in range(1, groups):
        pl.semaphore_signal(
            barrier, inc=1, device_id={"seq": lax.rem(me + step, groups)}, device_id_type=pl.DeviceIdType.MESH
        )
    for step in range(1, peers):
        pl.semaphore_signal(
            barrier, inc=1, device_id={"chan": lax.rem(row + step, peers)}, device_id_type=pl.DeviceIdType.MESH
        )
    own_hidden = local(hidden_hbm, hidden, own_sem.at[1])
    own_gate = local(gate_hbm, gate_in, own_sem.at[2])
    own_filters = [
        local(
            filters.at[pl.ds(pl.multiple_of(me * count + part * sub, sub), sub), :],
            filter_in.at[part, me],
            own_sem.at[3 + parts + part],
        )
        for part in range(parts)
    ]
    tables = [
        local(source, target, table_sem.at[index])
        for index, (source, target) in enumerate(((fwd_hi, fh), (fwd_lo, fl), (inv_hi, ih), (inv_lo, il)))
    ]
    own_hidden.wait()
    partial = jnp.zeros((1, width), jnp.float32)
    for block in range(groups):
        activity = hidden[block * count : (block + 1) * count, :].astype(jnp.float32)
        partial = partial + jnp.sum(activity * activity, axis=0, keepdims=True)
    local_sum[...] = partial
    sums[row] = partial
    pl.semaphore_wait(barrier, groups + peers - 2)

    order = [groups // 2] + [s for s in range(1, groups) if s != groups // 2]

    def send_filters(part):
        return [
            send(
                part * groups + step,
                step,
                filters.at[pl.ds(pl.multiple_of(lax.rem(me + step, groups) * count + part * sub, sub), sub), :],
                filter_in.at[part, me],
                f_send,
                f_recv,
            )
            for step in range(1, groups)
        ]

    def gated(block, part):
        rows = pl.ds(pl.multiple_of(block * count + part * sub, sub), sub)
        gains = column(gain[block], count, width)[part * sub : (part + 1) * sub]
        return gate_in[rows, :].astype(jnp.float32) * (hidden[rows, :].astype(jnp.float32) * gains)

    def send_signal(part):
        copies = []
        for step in range(1, groups):
            to = lax.rem(me + step, groups)
            signal[part, to] = gated(to, part)
            copies.append(
                send(part * groups + step, step, signal.at[part, to], signal_in.at[part, me], s_send, s_recv)
            )
        signal_in[part, me] = gated(me, part)
        return copies

    filter_copies = [send_filters(0)]
    sum_copies = []
    for step in range(1, peers):
        copy = pltpu.make_async_remote_copy(
            src_ref=local_sum, dst_ref=sums.at[row], send_sem=q_send.at[step], recv_sem=q_recv.at[step],
            device_id={"chan": lax.rem(row + step, peers)}, device_id_type=pl.DeviceIdType.MESH,
        )
        copy.start()
        sum_copies.append(copy)
    own_gate.wait()
    signal_copies = [send_signal(0)]
    for part in range(1, parts):
        filter_copies.append(send_filters(part))
    for copy in sum_copies:
        copy.wait()
    total = sums[0]
    for index in range(1, peers):
        total = total + sums[index]
    scale = lax.rsqrt(total / (hidden.shape[0] * peers) + epsilon)
    scale_out[...] = scale
    scales[me] = scale
    scale_copies = [send(step, step, scales.at[me], scales.at[me], r_send, r_recv) for step in range(1, groups)]
    for part in range(1, parts):
        signal_copies.append(send_signal(part))

    chunks = fh.shape[0]
    chunk = fh.shape[2] // 2

    def store_halves(block, value):
        high, low = halves(value)
        halved[:sub, block * width : (block + 1) * width] = high
        halved[sub:, block * width : (block + 1) * width] = low

    def transform(index):
        both = jnp.dot(halved[...], fh[index], preferred_element_type=jnp.float32)
        small = jnp.dot(halved[:sub, :], fl[index], preferred_element_type=jnp.float32)
        return both[:sub] + (both[sub:] + small)

    def filter_step(index, carry):
        spectrum[index] = transform(index)
        return carry

    def invert(block):
        both = jnp.dot(product[...], ih[block], preferred_element_type=jnp.float32)
        small = jnp.dot(product[:sub, :], il[block], preferred_element_type=jnp.float32)
        return both[:sub] + (both[sub:] + small)

    for copy in own_filters:
        copy.wait()
    conv_copies = []
    for part in range(parts):
        for copy in filter_copies[part]:
            copy.wait()
        for block in range(groups):
            store_halves(block, filter_in[part, block])
        if part == 0:
            tables[0].wait()
            tables[1].wait()
        lax.fori_loop(0, chunks, filter_step, 0)
        for copy in signal_copies[part]:
            copy.wait()
        if part == 0:
            for copy in scale_copies:
                copy.wait()
        for block in range(groups):
            store_halves(block, signal_in[part, block] * scales[block])
        for index in range(chunks):
            s_both = transform(index)
            s_real, s_imag = s_both[:, :chunk], s_both[:, chunk:]
            f_both = spectrum[index]
            f_real, f_imag = f_both[:, :chunk], f_both[:, chunk:]
            real_high, real_low = halves(s_real * f_real - s_imag * f_imag)
            imag_high, imag_low = halves(s_real * f_imag + s_imag * f_real)
            start = 2 * index * chunk
            product[:sub, start : start + chunk] = real_high
            product[sub:, start : start + chunk] = real_low
            product[:sub, start + chunk : start + 2 * chunk] = imag_high
            product[sub:, start + chunk : start + 2 * chunk] = imag_low
        if part == 0:
            tables[2].wait()
            tables[3].wait()
        for step in order:
            to = lax.rem(me + step, groups)
            conv_out[part, to] = invert(to)
            conv_copies.append(
                send(part * groups + step, step, conv_out.at[part, to], conv_in.at[me, part], c_send, c_recv)
            )
        conv_out[part, me] = invert(me)
        conv_copies.append(local(conv_out.at[part, me], conv_in.at[me, part], own_sem.at[3 + part]))
    for copy in conv_copies:
        copy.wait()


def fused(hidden, gate_in, gate_out, filters, norm_gain, skip_weight):
    channels, width = hidden.shape
    groups, peers = lax.axis_size("seq"), lax.axis_size("chan")
    length, count = groups * width, channels // groups
    chunk = min(256, length)
    tables = [jnp.asarray(t) for t in transform_tables(length, chunk, groups)]
    vmem = pl.BlockSpec(memory_space=pltpu.VMEM)
    hbm = pl.BlockSpec(memory_space=pl.ANY)
    parts = 2
    sub = count // parts
    block = (parts, groups, sub, width)
    f32, bf16 = jnp.float32, jnp.bfloat16
    pair = pltpu.SemaphoreType.DMA((parts * groups,))
    ring = pltpu.SemaphoreType.DMA((peers,))
    conv, scale = pl.pallas_call(
        functools.partial(conv_kernel, groups, peers),
        out_shape=[jax.ShapeDtypeStruct((groups, parts, sub, width), f32), jax.ShapeDtypeStruct((1, width), f32)],
        in_specs=[hbm, hbm, hbm, vmem, hbm, hbm, hbm, hbm],
        out_specs=[hbm, vmem],
        scratch_shapes=[
            pltpu.VMEM(tables[0].shape, bf16),
            pltpu.VMEM(tables[1].shape, bf16),
            pltpu.VMEM(tables[2].shape, bf16),
            pltpu.VMEM(tables[3].shape, bf16),
            pltpu.VMEM((channels, width), bf16),
            pltpu.VMEM((channels, width), bf16),
            pltpu.VMEM(block, f32),
            pltpu.VMEM(block, f32),
            pltpu.VMEM(block, f32),
            pltpu.VMEM(block, f32),
            pltpu.VMEM((1, width), f32),
            pltpu.VMEM((peers, 1, width), f32),
            pltpu.VMEM((groups, 1, width), f32),
            pltpu.VMEM((2 * sub, length), bf16),
            pltpu.VMEM((length // chunk, sub, 2 * chunk), f32),
            pltpu.VMEM((2 * sub, 2 * length), bf16),
            pltpu.SemaphoreType.DMA((4,)),
            pltpu.SemaphoreType.DMA((3 + 2 * parts,)),
            pair, pair, pair, pair, pair, pair, pair, pair, ring, ring,
        ],
        compiler_params=pltpu.CompilerParams(
            collective_id=0, has_side_effects=True, vmem_limit_bytes=56 * 1024 * 1024
        ),
    )(hidden, gate_in, filters, norm_gain.reshape(groups, 1, count), *tables)
    signal = gate_in.astype(f32) * (hidden.astype(f32) * norm_gain[:, None]) * scale
    mixed = gate_out.astype(f32) * (conv.reshape(channels, width) + skip_weight[:, None] * signal)
    return mixed.astype(bf16)


def per_device(hidden, gate_in, gate_out, filters, norm_gain, skip_weight):
    length = hidden.shape[1] * lax.axis_size("seq")
    if 16 * length * length <= 2**24 and hidden.shape[0] == 128 * lax.axis_size("seq"):
        return fused(hidden, gate_in, gate_out, filters, norm_gain, skip_weight)
    activity = hidden.astype(jnp.float32)
    channels, positions = activity.shape
    squares = lax.psum(jnp.sum(activity * activity, axis=0), "chan")
    mean_sq = squares / (channels * lax.axis_size("chan")) + epsilon
    normed = activity * lax.rsqrt(mean_sq)[None, :] * norm_gain[:, None]
    signal = gate_in.astype(jnp.float32) * normed
    groups = lax.axis_size("seq")
    width = positions // groups
    period = 2 * positions * groups
    conv = four_step(signal, filters, groups, width, period)
    mixed = gate_out.astype(jnp.float32) * (conv + skip_weight[:, None] * signal)
    return mixed.astype(jnp.bfloat16)


def solution(mesh):
    placed = (
        P("chan", "seq"),
        P("chan", "seq"),
        P("chan", "seq"),
        P("chan", "seq"),
        P("chan"),
        P("chan"),
    )
    return jax.shard_map(
        per_device, mesh=mesh, in_specs=placed, out_specs=P("chan", "seq"), check_vma=False
    )
```

```python
import functools
import math

import jax
import jax.numpy as jnp
import numpy as np
from jax import lax
from jax.experimental import pallas as pl
from jax.experimental.pallas import tpu as pltpu
from jax.sharding import PartitionSpec as P

highest = lax.Precision.HIGHEST
epsilon = 1e-06


def angle_table(row_count, col_count, period, sign):
    row_index = lax.iota(jnp.int32, row_count)[:, None]
    col_index = lax.iota(jnp.int32, col_count)[None, :]
    phase = (row_index * col_index % period).astype(jnp.float32) * (2.0 * math.pi / period)
    return (jnp.cos(phase), sign * jnp.sin(phase))


def twiddle_table(row_count, col_count, span, offset, period, sign):
    row_index = lax.iota(jnp.int32, row_count)[:, None]
    col_index = (lax.iota(jnp.int32, col_count) % span + offset)[None, :]
    phase = (row_index * col_index % period).astype(jnp.float32) * (2.0 * math.pi / period)
    return (jnp.cos(phase), sign * jnp.sin(phase))


def rotate(left_real, left_imag, right_real, right_imag):
    return (
        left_real * right_real - left_imag * right_imag,
        left_real * right_imag + left_imag * right_real,
    )


def sequence_forward(block, groups, span, offset, period):
    rows = 2 * groups
    cosine, sine = angle_table(rows, groups, rows, -1.0)
    both = jnp.dot(jnp.concatenate([cosine, sine], axis=0), block, precision=highest)
    real_part, imag_part = (both[:rows], both[rows:])
    turn_real, turn_imag = twiddle_table(rows, block.shape[1], span, offset, period, -1.0)
    return rotate(real_part, imag_part, turn_real, turn_imag)


def sequence_inverse(real_part, imag_part, groups, span, offset, period):
    rows = 2 * groups
    turn_real, turn_imag = twiddle_table(rows, real_part.shape[1], span, offset, period, 1.0)
    real_part, imag_part = rotate(real_part, imag_part, turn_real, turn_imag)
    cosine, sine = angle_table(groups, rows, rows, 1.0)
    return jnp.dot(cosine, real_part, precision=highest) - jnp.dot(
        sine, imag_part, precision=highest
    )


def full_transform(stacked, sign):
    length = stacked.shape[1]
    cosine, sine = angle_table(length, length, length, sign)
    return jnp.dot(stacked, jnp.concatenate([cosine, sine], axis=1), precision=highest)


def spectral_product(signal_real, signal_imag, filter_real, filter_imag):
    count, length = signal_real.shape
    stacked = jnp.concatenate([signal_real, signal_imag, filter_real, filter_imag], axis=0)
    spectra = full_transform(stacked, -1.0)
    s_real = spectra[:count, :length] - spectra[count : 2 * count, length:]
    s_imag = spectra[:count, length:] + spectra[count : 2 * count, :length]
    f_real = spectra[2 * count : 3 * count, :length] - spectra[3 * count :, length:]
    f_imag = spectra[2 * count : 3 * count, length:] + spectra[3 * count :, :length]
    product_real, product_imag = rotate(s_real, s_imag, f_real, f_imag)
    back = full_transform(jnp.concatenate([product_real, product_imag], axis=0), 1.0)
    return (
        back[:count, :length] - back[count:, length:],
        back[:count, length:] + back[count:, :length],
    )


def four_step(signal, filters, groups, width, period):
    channels, positions = signal.shape
    spread_signal, spread_filter = (
        lax.all_to_all(signal, "seq", split_axis=1, concat_axis=0, tiled=True),
        lax.all_to_all(filters, "seq", split_axis=1, concat_axis=0, tiled=True),
    )
    flat = (groups, channels * width)
    offset = lax.axis_index("seq") * width
    signal_real, signal_imag = sequence_forward(
        spread_signal.reshape(flat), groups, width, offset, period
    )
    filter_real, filter_imag = sequence_forward(
        spread_filter.reshape(flat), groups, width, offset, period
    )
    middle = (2 * groups, channels, width)
    signal_real, signal_imag, filter_real, filter_imag = (
        lax.all_to_all(signal_real.reshape(middle), "seq", split_axis=0, concat_axis=2, tiled=True),
        lax.all_to_all(signal_imag.reshape(middle), "seq", split_axis=0, concat_axis=2, tiled=True),
        lax.all_to_all(filter_real.reshape(middle), "seq", split_axis=0, concat_axis=2, tiled=True),
        lax.all_to_all(filter_imag.reshape(middle), "seq", split_axis=0, concat_axis=2, tiled=True),
    )
    rows = (2 * channels, positions)
    back_real, back_imag = spectral_product(
        signal_real.reshape(rows),
        signal_imag.reshape(rows),
        filter_real.reshape(rows),
        filter_imag.reshape(rows),
    )
    split = (2, channels, positions)
    back_real, back_imag = (
        lax.all_to_all(back_real.reshape(split), "seq", split_axis=2, concat_axis=0, tiled=True),
        lax.all_to_all(back_imag.reshape(split), "seq", split_axis=2, concat_axis=0, tiled=True),
    )
    wide = (2 * groups, channels * width)
    field = sequence_inverse(
        back_real.reshape(wide), back_imag.reshape(wide), groups, width, offset, period
    )
    result = lax.all_to_all(
        field.reshape(groups, channels, width), "seq", split_axis=0, concat_axis=2, tiled=True
    )
    return result.reshape(channels, positions) / period


def split_table(table):
    high = table.astype(jnp.bfloat16)
    low = (table - high.astype(np.float64)).astype(jnp.bfloat16)
    return high, low


def transform_tables(length, chunk, blocks):
    place = np.arange(length)[:, None]
    odd = 2 * np.arange(length)[None, :] + 1
    phase = (place * odd % (4 * length)) * (2.0 * np.pi / (4 * length))
    chunks = length // chunk
    cosine = np.cos(phase).reshape(length, chunks, chunk)
    sine = np.sin(phase).reshape(length, chunks, chunk)
    both = np.concatenate([cosine, -sine], axis=2)
    forward = both.transpose(1, 0, 2)
    inverse = both.reshape(length, 2 * length).T / length
    inverse = inverse.reshape(2 * length, blocks, length // blocks).transpose(1, 0, 2)
    return split_table(forward) + split_table(inverse)


def halves(value):
    high = value.astype(jnp.bfloat16)
    return high, (value - high.astype(jnp.float32)).astype(jnp.bfloat16)


def column(row, count, width):
    square = jnp.transpose(jnp.broadcast_to(row, (128, count)))
    return jnp.concatenate([square] * (width // 128), axis=1)


def conv_kernel(
    groups, peers, hidden_hbm, gate_hbm, filters, gain, fwd_hi, fwd_lo, inv_hi, inv_lo,
    conv_in, scale_out,
    fh, fl, ih, il, hidden, gate_in, filter_in, signal_in, conv_out, signal, local_sum, sums, halved_filter, halved, spectrum,
    product,
    table_sem, own_sem, f_send, f_recv, s_send, s_recv, c_send, c_recv, q_send, q_recv,
):
    me = lax.axis_index("seq")
    row = lax.axis_index("chan")
    count = hidden.shape[0] // groups
    width = hidden.shape[1]
    parts = signal_in.shape[0]
    sub = count // parts

    def local(source, target, sem):
        copy = pltpu.make_async_copy(source, target, sem)
        copy.start()
        return copy

    def send(slot, step, source, target, sent, received):
        copy = pltpu.make_async_remote_copy(
            src_ref=source, dst_ref=target, send_sem=sent.at[slot], recv_sem=received.at[slot],
            device_id={"seq": lax.rem(me + step, groups)}, device_id_type=pl.DeviceIdType.MESH,
        )
        copy.start()
        return copy

    barrier = pltpu.get_barrier_semaphore()
    for step in range(1, groups):
        pl.semaphore_signal(
            barrier, inc=1, device_id={"seq": lax.rem(me + step, groups)}, device_id_type=pl.DeviceIdType.MESH
        )
    for step in range(1, peers):
        pl.semaphore_signal(
            barrier, inc=1, device_id={"chan": lax.rem(row + step, peers)}, device_id_type=pl.DeviceIdType.MESH
        )
    own_hidden = local(hidden_hbm, hidden, own_sem.at[1])
    own_gate = local(gate_hbm, gate_in, own_sem.at[2])
    own_filter = local(
        filters.at[pl.ds(pl.multiple_of(me * count, count), count), :], filter_in.at[me], own_sem.at[0]
    )
    tables = [
        local(source, target, table_sem.at[index])
        for index, (source, target) in enumerate(((fwd_hi, fh), (fwd_lo, fl), (inv_hi, ih), (inv_lo, il)))
    ]
    own_hidden.wait()
    partial = jnp.zeros((1, width), jnp.float32)
    for block in range(groups):
        activity = hidden[block * count : (block + 1) * count, :].astype(jnp.float32)
        partial = partial + jnp.sum(activity * activity, axis=0, keepdims=True)
    local_sum[...] = partial
    sums[row] = partial
    pl.semaphore_wait(barrier, groups + peers - 2)

    order = [groups // 2] + [s for s in range(1, groups) if s != groups // 2]

    filter_copies = [
        send(
            step,
            step,
            filters.at[pl.ds(pl.multiple_of(lax.rem(me + step, groups) * count, count), count), :],
            filter_in.at[me],
            f_send,
            f_recv,
        )
        for step in range(1, groups)
    ]
    sum_copies = []
    for step in range(1, peers):
        copy = pltpu.make_async_remote_copy(
            src_ref=local_sum, dst_ref=sums.at[row], send_sem=q_send.at[step], recv_sem=q_recv.at[step],
            device_id={"chan": lax.rem(row + step, peers)}, device_id_type=pl.DeviceIdType.MESH,
        )
        copy.start()
        sum_copies.append(copy)
    own_gate.wait()
    for block in range(groups):
        gains = column(gain[block], count, width)
        for part in range(parts):
            rows = slice(block * count + part * sub, block * count + (part + 1) * sub)
            scaled = hidden[rows, :].astype(jnp.float32) * gains[part * sub : (part + 1) * sub]
            signal[part, block] = gate_in[rows, :].astype(jnp.float32) * scaled
    for copy in sum_copies:
        copy.wait()
    total = sums[0]
    for index in range(1, peers):
        total = total + sums[index]
    scale = lax.rsqrt(total / (hidden.shape[0] * peers) + epsilon)
    signal_copies = []
    for part in range(parts):
        copies = []
        for step in range(1, groups):
            to = lax.rem(me + step, groups)
            signal[part, to] = signal[part, to] * scale
            copies.append(
                send(part * groups + step, step, signal.at[part, to], signal_in.at[part, me], s_send, s_recv)
            )
        signal_in[part, me] = signal[part, me] * scale
        signal_copies.append(copies)
    scale_out[...] = scale

    chunks = fh.shape[0]
    chunk = fh.shape[2] // 2

    def store_halves(target, block, value):
        size = value.shape[0]
        high, low = halves(value)
        target[:size, block * width : (block + 1) * width] = high
        target[size:, block * width : (block + 1) * width] = low

    def transform(source, index):
        size = source.shape[0] // 2
        both = jnp.dot(source[...], fh[index], preferred_element_type=jnp.float32)
        small = jnp.dot(source[:size, :], fl[index], preferred_element_type=jnp.float32)
        return both[:size] + (both[size:] + small)

    def filter_step(index, carry):
        spectrum[index] = transform(halved_filter, index)
        return carry

    def invert(block):
        both = jnp.dot(product[...], ih[block], preferred_element_type=jnp.float32)
        small = jnp.dot(product[:sub, :], il[block], preferred_element_type=jnp.float32)
        return both[:sub] + (both[sub:] + small)

    own_filter.wait()
    for copy in filter_copies:
        copy.wait()
    for block in range(groups):
        store_halves(halved_filter, block, filter_in[block])
    tables[0].wait()
    tables[1].wait()
    lax.fori_loop(0, chunks, filter_step, 0)
    conv_copies = []
    for part in range(parts):
        for copy in signal_copies[part]:
            copy.wait()
        for block in range(groups):
            store_halves(halved, block, signal_in[part, block])
        for index in range(chunks):
            s_both = transform(halved, index)
            s_real, s_imag = s_both[:, :chunk], s_both[:, chunk:]
            f_both = spectrum[index][part * sub : (part + 1) * sub]
            f_real, f_imag = f_both[:, :chunk], f_both[:, chunk:]
            real_high, real_low = halves(s_real * f_real - s_imag * f_imag)
            imag_high, imag_low = halves(s_real * f_imag + s_imag * f_real)
            start = 2 * index * chunk
            product[:sub, start : start + chunk] = real_high
            product[sub:, start : start + chunk] = real_low
            product[:sub, start + chunk : start + 2 * chunk] = imag_high
            product[sub:, start + chunk : start + 2 * chunk] = imag_low
        if part == 0:
            tables[2].wait()
            tables[3].wait()
        for step in order:
            to = lax.rem(me + step, groups)
            conv_out[part, to] = invert(to)
            conv_copies.append(
                send(part * groups + step, step, conv_out.at[part, to], conv_in.at[me, part], c_send, c_recv)
            )
        conv_out[part, me] = invert(me)
        conv_copies.append(local(conv_out.at[part, me], conv_in.at[me, part], own_sem.at[3 + part]))
    for copy in conv_copies:
        copy.wait()


def fused(hidden, gate_in, gate_out, filters, norm_gain, skip_weight):
    channels, width = hidden.shape
    groups, peers = lax.axis_size("seq"), lax.axis_size("chan")
    length, count = groups * width, channels // groups
    chunk = min(256, length)
    tables = [jnp.asarray(t) for t in transform_tables(length, chunk, groups)]
    vmem = pl.BlockSpec(memory_space=pltpu.VMEM)
    hbm = pl.BlockSpec(memory_space=pl.ANY)
    parts = 2
    sub = count // parts
    block = (parts, groups, sub, width)
    f32, bf16 = jnp.float32, jnp.bfloat16
    pair = pltpu.SemaphoreType.DMA((parts * groups,))
    ring = pltpu.SemaphoreType.DMA((peers,))
    conv, scale = pl.pallas_call(
        functools.partial(conv_kernel, groups, peers),
        out_shape=[jax.ShapeDtypeStruct((groups, parts, sub, width), f32), jax.ShapeDtypeStruct((1, width), f32)],
        in_specs=[hbm, hbm, hbm, vmem, hbm, hbm, hbm, hbm],
        out_specs=[hbm, vmem],
        scratch_shapes=[
            pltpu.VMEM(tables[0].shape, bf16),
            pltpu.VMEM(tables[1].shape, bf16),
            pltpu.VMEM(tables[2].shape, bf16),
            pltpu.VMEM(tables[3].shape, bf16),
            pltpu.VMEM((channels, width), bf16),
            pltpu.VMEM((channels, width), bf16),
            pltpu.VMEM((groups, count, width), f32),
            pltpu.VMEM(block, f32),
            pltpu.VMEM(block, f32),
            pltpu.VMEM(block, f32),
            pltpu.VMEM((1, width), f32),
            pltpu.VMEM((peers, 1, width), f32),
            pltpu.VMEM((2 * count, length), bf16),
            pltpu.VMEM((2 * sub, length), bf16),
            pltpu.VMEM((length // chunk, count, 2 * chunk), f32),
            pltpu.VMEM((2 * sub, 2 * length), bf16),
            pltpu.SemaphoreType.DMA((4,)),
            pltpu.SemaphoreType.DMA((3 + parts,)),
            pair, pair, pair, pair, pair, pair, ring, ring,
        ],
        compiler_params=pltpu.CompilerParams(
            collective_id=0, has_side_effects=True, vmem_limit_bytes=56 * 1024 * 1024
        ),
    )(hidden, gate_in, filters, norm_gain.reshape(groups, 1, count), *tables)
    signal = gate_in.astype(f32) * (hidden.astype(f32) * norm_gain[:, None]) * scale
    mixed = gate_out.astype(f32) * (conv.reshape(channels, width) + skip_weight[:, None] * signal)
    return mixed.astype(bf16)


def per_device(hidden, gate_in, gate_out, filters, norm_gain, skip_weight):
    length = hidden.shape[1] * lax.axis_size("seq")
    if 16 * length * length <= 2**24 and hidden.shape[0] == 128 * lax.axis_size("seq"):
        return fused(hidden, gate_in, gate_out, filters, norm_gain, skip_weight)
    activity = hidden.astype(jnp.float32)
    channels, positions = activity.shape
    squares = lax.psum(jnp.sum(activity * activity, axis=0), "chan")
    mean_sq = squares / (channels * lax.axis_size("chan")) + epsilon
    normed = activity * lax.rsqrt(mean_sq)[None, :] * norm_gain[:, None]
    signal = gate_in.astype(jnp.float32) * normed
    groups = lax.axis_size("seq")
    width = positions // groups
    period = 2 * positions * groups
    conv = four_step(signal, filters, groups, width, period)
    mixed = gate_out.astype(jnp.float32) * (conv + skip_weight[:, None] * signal)
    return mixed.astype(jnp.bfloat16)


def solution(mesh):
    placed = (
        P("chan", "seq"),
        P("chan", "seq"),
        P("chan", "seq"),
        P("chan", "seq"),
        P("chan"),
        P("chan"),
    )
    return jax.shard_map(
        per_device, mesh=mesh, in_specs=placed, out_specs=P("chan", "seq"), check_vma=False
    )
```

```python
import functools
import math

import jax
import jax.numpy as jnp
import numpy as np
from jax import lax
from jax.experimental import pallas as pl
from jax.experimental.pallas import tpu as pltpu
from jax.sharding import PartitionSpec as P

highest = lax.Precision.HIGHEST
epsilon = 1e-06


def angle_table(row_count, col_count, period, sign):
    row_index = lax.iota(jnp.int32, row_count)[:, None]
    col_index = lax.iota(jnp.int32, col_count)[None, :]
    phase = (row_index * col_index % period).astype(jnp.float32) * (2.0 * math.pi / period)
    return (jnp.cos(phase), sign * jnp.sin(phase))


def twiddle_table(row_count, col_count, span, offset, period, sign):
    row_index = lax.iota(jnp.int32, row_count)[:, None]
    col_index = (lax.iota(jnp.int32, col_count) % span + offset)[None, :]
    phase = (row_index * col_index % period).astype(jnp.float32) * (2.0 * math.pi / period)
    return (jnp.cos(phase), sign * jnp.sin(phase))


def rotate(left_real, left_imag, right_real, right_imag):
    return (
        left_real * right_real - left_imag * right_imag,
        left_real * right_imag + left_imag * right_real,
    )


def sequence_forward(block, groups, span, offset, period):
    rows = 2 * groups
    cosine, sine = angle_table(rows, groups, rows, -1.0)
    both = jnp.dot(jnp.concatenate([cosine, sine], axis=0), block, precision=highest)
    real_part, imag_part = (both[:rows], both[rows:])
    turn_real, turn_imag = twiddle_table(rows, block.shape[1], span, offset, period, -1.0)
    return rotate(real_part, imag_part, turn_real, turn_imag)


def sequence_inverse(real_part, imag_part, groups, span, offset, period):
    rows = 2 * groups
    turn_real, turn_imag = twiddle_table(rows, real_part.shape[1], span, offset, period, 1.0)
    real_part, imag_part = rotate(real_part, imag_part, turn_real, turn_imag)
    cosine, sine = angle_table(groups, rows, rows, 1.0)
    return jnp.dot(cosine, real_part, precision=highest) - jnp.dot(
        sine, imag_part, precision=highest
    )


def full_transform(stacked, sign):
    length = stacked.shape[1]
    cosine, sine = angle_table(length, length, length, sign)
    return jnp.dot(stacked, jnp.concatenate([cosine, sine], axis=1), precision=highest)


def spectral_product(signal_real, signal_imag, filter_real, filter_imag):
    count, length = signal_real.shape
    stacked = jnp.concatenate([signal_real, signal_imag, filter_real, filter_imag], axis=0)
    spectra = full_transform(stacked, -1.0)
    s_real = spectra[:count, :length] - spectra[count : 2 * count, length:]
    s_imag = spectra[:count, length:] + spectra[count : 2 * count, :length]
    f_real = spectra[2 * count : 3 * count, :length] - spectra[3 * count :, length:]
    f_imag = spectra[2 * count : 3 * count, length:] + spectra[3 * count :, :length]
    product_real, product_imag = rotate(s_real, s_imag, f_real, f_imag)
    back = full_transform(jnp.concatenate([product_real, product_imag], axis=0), 1.0)
    return (
        back[:count, :length] - back[count:, length:],
        back[:count, length:] + back[count:, :length],
    )


def four_step(signal, filters, groups, width, period):
    channels, positions = signal.shape
    spread_signal, spread_filter = (
        lax.all_to_all(signal, "seq", split_axis=1, concat_axis=0, tiled=True),
        lax.all_to_all(filters, "seq", split_axis=1, concat_axis=0, tiled=True),
    )
    flat = (groups, channels * width)
    offset = lax.axis_index("seq") * width
    signal_real, signal_imag = sequence_forward(
        spread_signal.reshape(flat), groups, width, offset, period
    )
    filter_real, filter_imag = sequence_forward(
        spread_filter.reshape(flat), groups, width, offset, period
    )
    middle = (2 * groups, channels, width)
    signal_real, signal_imag, filter_real, filter_imag = (
        lax.all_to_all(signal_real.reshape(middle), "seq", split_axis=0, concat_axis=2, tiled=True),
        lax.all_to_all(signal_imag.reshape(middle), "seq", split_axis=0, concat_axis=2, tiled=True),
        lax.all_to_all(filter_real.reshape(middle), "seq", split_axis=0, concat_axis=2, tiled=True),
        lax.all_to_all(filter_imag.reshape(middle), "seq", split_axis=0, concat_axis=2, tiled=True),
    )
    rows = (2 * channels, positions)
    back_real, back_imag = spectral_product(
        signal_real.reshape(rows),
        signal_imag.reshape(rows),
        filter_real.reshape(rows),
        filter_imag.reshape(rows),
    )
    split = (2, channels, positions)
    back_real, back_imag = (
        lax.all_to_all(back_real.reshape(split), "seq", split_axis=2, concat_axis=0, tiled=True),
        lax.all_to_all(back_imag.reshape(split), "seq", split_axis=2, concat_axis=0, tiled=True),
    )
    wide = (2 * groups, channels * width)
    field = sequence_inverse(
        back_real.reshape(wide), back_imag.reshape(wide), groups, width, offset, period
    )
    result = lax.all_to_all(
        field.reshape(groups, channels, width), "seq", split_axis=0, concat_axis=2, tiled=True
    )
    return result.reshape(channels, positions) / period


def split_table(table):
    high = table.astype(jnp.bfloat16)
    low = (table - high.astype(np.float64)).astype(jnp.bfloat16)
    return high, low


def transform_tables(length, chunk, blocks):
    place = np.arange(length)[:, None]
    odd = 2 * np.arange(length)[None, :] + 1
    phase = (place * odd % (4 * length)) * (2.0 * np.pi / (4 * length))
    chunks = length // chunk
    cosine = np.cos(phase).reshape(length, chunks, chunk)
    sine = np.sin(phase).reshape(length, chunks, chunk)
    both = np.concatenate([cosine, -sine], axis=2)
    forward = both.transpose(1, 0, 2)
    inverse = both.reshape(length, 2 * length).T / length
    inverse = inverse.reshape(2 * length, blocks, length // blocks).transpose(1, 0, 2)
    return split_table(forward) + split_table(inverse)


def halves(value):
    high = value.astype(jnp.bfloat16)
    return high, (value - high.astype(jnp.float32)).astype(jnp.bfloat16)


def column(row, count, width):
    square = jnp.transpose(jnp.broadcast_to(row, (128, count)))
    return jnp.concatenate([square] * (width // 128), axis=1)


def conv_kernel(
    groups, peers, hidden_hbm, gate_hbm, filters, gain, skip, fwd_hi, fwd_lo, inv_hi, inv_lo,
    conv_in,
    fh, fl, ih, il, hidden, gate_in, filter_in, signal_in, conv_out, signal, local_sum, sums, halved_filter, halved, spectrum,
    product,
    table_sem, own_sem, f_send, f_recv, s_send, s_recv, c_send, c_recv, q_send, q_recv,
):
    me = lax.axis_index("seq")
    row = lax.axis_index("chan")
    count = hidden.shape[0] // groups
    width = hidden.shape[1]
    parts = signal_in.shape[0]
    sub = count // parts

    def local(source, target, sem):
        copy = pltpu.make_async_copy(source, target, sem)
        copy.start()
        return copy

    def send(slot, step, source, target, sent, received):
        copy = pltpu.make_async_remote_copy(
            src_ref=source, dst_ref=target, send_sem=sent.at[slot], recv_sem=received.at[slot],
            device_id={"seq": lax.rem(me + step, groups)}, device_id_type=pl.DeviceIdType.MESH,
        )
        copy.start()
        return copy

    barrier = pltpu.get_barrier_semaphore()
    for step in range(1, peers):
        pl.semaphore_signal(
            barrier, inc=1, device_id={"chan": lax.rem(row + step, peers)}, device_id_type=pl.DeviceIdType.MESH
        )
    for step in range(1, groups):
        pl.semaphore_signal(
            barrier, inc=1, device_id={"seq": lax.rem(me + step, groups)}, device_id_type=pl.DeviceIdType.MESH
        )
    own_hidden = local(hidden_hbm, hidden, own_sem.at[1])
    own_gate = local(gate_hbm, gate_in, own_sem.at[2])
    own_filter = local(
        filters.at[pl.ds(pl.multiple_of(me * count, count), count), :], filter_in.at[me], own_sem.at[0]
    )
    tables = [
        local(source, target, table_sem.at[index])
        for index, (source, target) in enumerate(((fwd_hi, fh), (fwd_lo, fl), (inv_hi, ih), (inv_lo, il)))
    ]
    own_hidden.wait()
    partial = jnp.zeros((1, width), jnp.float32)
    for block in range(groups):
        activity = hidden[block * count : (block + 1) * count, :].astype(jnp.float32)
        partial = partial + jnp.sum(activity * activity, axis=0, keepdims=True)
    local_sum[...] = partial
    sums[row] = partial
    pl.semaphore_wait(barrier, groups + peers - 2)

    order = [groups // 2] + [s for s in range(1, groups) if s != groups // 2]

    filter_copies = [
        send(
            step,
            step,
            filters.at[pl.ds(pl.multiple_of(lax.rem(me + step, groups) * count, count), count), :],
            filter_in.at[me],
            f_send,
            f_recv,
        )
        for step in range(1, groups)
    ]
    sum_copies = []
    for step in range(1, peers):
        copy = pltpu.make_async_remote_copy(
            src_ref=local_sum, dst_ref=sums.at[row], send_sem=q_send.at[step], recv_sem=q_recv.at[step],
            device_id={"chan": lax.rem(row + step, peers)}, device_id_type=pl.DeviceIdType.MESH,
        )
        copy.start()
        sum_copies.append(copy)
    own_gate.wait()
    for block in range(groups):
        gains = column(gain[block], count, width)
        for part in range(parts):
            rows = slice(block * count + part * sub, block * count + (part + 1) * sub)
            scaled = hidden[rows, :].astype(jnp.float32) * gains[part * sub : (part + 1) * sub]
            signal[part, block] = gate_in[rows, :].astype(jnp.float32) * scaled
    for copy in sum_copies:
        copy.wait()
    total = sums[0]
    for index in range(1, peers):
        total = total + sums[index]
    scale = lax.rsqrt(total / (hidden.shape[0] * peers) + epsilon)
    signal_copies = []
    for part in range(parts):
        copies = []
        for step in range(1, groups):
            to = lax.rem(me + step, groups)
            signal[part, to] = signal[part, to] * scale
            copies.append(
                send(part * groups + step, step, signal.at[part, to], signal_in.at[part, me], s_send, s_recv)
            )
        signal_in[part, me] = signal[part, me] * scale
        signal_copies.append(copies)

    chunks = fh.shape[0]
    chunk = fh.shape[2] // 2

    def store_halves(target, block, value):
        size = value.shape[0]
        high, low = halves(value)
        target[:size, block * width : (block + 1) * width] = high
        target[size:, block * width : (block + 1) * width] = low

    def transform(source, index):
        size = source.shape[0] // 2
        both = jnp.dot(source[...], fh[index], preferred_element_type=jnp.float32)
        small = jnp.dot(source[:size, :], fl[index], preferred_element_type=jnp.float32)
        return both[:size] + (both[size:] + small)

    def filter_step(index, carry):
        spectrum[index] = transform(halved_filter, index)
        return carry

    weights = column(skip[me], count, width)

    def invert(part, block):
        both = jnp.dot(product[...], ih[block], preferred_element_type=jnp.float32)
        small = jnp.dot(product[:sub, :], il[block], preferred_element_type=jnp.float32)
        conv = both[:sub] + (both[sub:] + small)
        return conv + weights[part * sub : (part + 1) * sub] * signal_in[part, block]

    own_filter.wait()
    for copy in filter_copies:
        copy.wait()
    for block in range(groups):
        store_halves(halved_filter, block, filter_in[block])
    tables[0].wait()
    tables[1].wait()
    lax.fori_loop(0, chunks, filter_step, 0)
    conv_copies = []
    for part in range(parts):
        for copy in signal_copies[part]:
            copy.wait()
        for block in range(groups):
            store_halves(halved, block, signal_in[part, block])
        for index in range(chunks):
            s_both = transform(halved, index)
            s_real, s_imag = s_both[:, :chunk], s_both[:, chunk:]
            f_both = spectrum[index][part * sub : (part + 1) * sub]
            f_real, f_imag = f_both[:, :chunk], f_both[:, chunk:]
            real_high, real_low = halves(s_real * f_real - s_imag * f_imag)
            imag_high, imag_low = halves(s_real * f_imag + s_imag * f_real)
            start = 2 * index * chunk
            product[:sub, start : start + chunk] = real_high
            product[sub:, start : start + chunk] = real_low
            product[:sub, start + chunk : start + 2 * chunk] = imag_high
            product[sub:, start + chunk : start + 2 * chunk] = imag_low
        if part == 0:
            tables[2].wait()
            tables[3].wait()
        for step in order:
            to = lax.rem(me + step, groups)
            conv_out[part, to] = invert(part, to)
            conv_copies.append(
                send(part * groups + step, step, conv_out.at[part, to], conv_in.at[me, part], c_send, c_recv)
            )
        conv_out[part, me] = invert(part, me)
        conv_copies.append(local(conv_out.at[part, me], conv_in.at[me, part], own_sem.at[3 + part]))
    for copy in conv_copies:
        copy.wait()


def fused(hidden, gate_in, gate_out, filters, norm_gain, skip_weight):
    channels, width = hidden.shape
    groups, peers = lax.axis_size("seq"), lax.axis_size("chan")
    length, count = groups * width, channels // groups
    chunk = min(256, length)
    tables = [jnp.asarray(t) for t in transform_tables(length, chunk, groups)]
    vmem = pl.BlockSpec(memory_space=pltpu.VMEM)
    hbm = pl.BlockSpec(memory_space=pl.ANY)
    parts = 2
    sub = count // parts
    block = (parts, groups, sub, width)
    f32, bf16 = jnp.float32, jnp.bfloat16
    pair = pltpu.SemaphoreType.DMA((parts * groups,))
    ring = pltpu.SemaphoreType.DMA((peers,))
    conv = pl.pallas_call(
        functools.partial(conv_kernel, groups, peers),
        out_shape=jax.ShapeDtypeStruct((groups, parts, sub, width), f32),
        in_specs=[hbm, hbm, hbm, vmem, vmem, hbm, hbm, hbm, hbm],
        out_specs=hbm,
        scratch_shapes=[
            pltpu.VMEM(tables[0].shape, bf16),
            pltpu.VMEM(tables[1].shape, bf16),
            pltpu.VMEM(tables[2].shape, bf16),
            pltpu.VMEM(tables[3].shape, bf16),
            pltpu.VMEM((channels, width), bf16),
            pltpu.VMEM((channels, width), bf16),
            pltpu.VMEM((groups, count, width), f32),
            pltpu.VMEM(block, f32),
            pltpu.VMEM(block, f32),
            pltpu.VMEM(block, f32),
            pltpu.VMEM((1, width), f32),
            pltpu.VMEM((peers, 1, width), f32),
            pltpu.VMEM((2 * count, length), bf16),
            pltpu.VMEM((2 * sub, length), bf16),
            pltpu.VMEM((length // chunk, count, 2 * chunk), f32),
            pltpu.VMEM((2 * sub, 2 * length), bf16),
            pltpu.SemaphoreType.DMA((4,)),
            pltpu.SemaphoreType.DMA((3 + parts,)),
            pair, pair, pair, pair, pair, pair, ring, ring,
        ],
        compiler_params=pltpu.CompilerParams(
            collective_id=0, has_side_effects=True, vmem_limit_bytes=56 * 1024 * 1024
        ),
    )(
        hidden, gate_in, filters,
        norm_gain.reshape(groups, 1, count), skip_weight.reshape(groups, 1, count), *tables,
    )
    mixed = gate_out.astype(f32) * conv.reshape(channels, width)
    return mixed.astype(bf16)


def per_device(hidden, gate_in, gate_out, filters, norm_gain, skip_weight):
    length = hidden.shape[1] * lax.axis_size("seq")
    if 16 * length * length <= 2**24 and hidden.shape[0] == 128 * lax.axis_size("seq"):
        return fused(hidden, gate_in, gate_out, filters, norm_gain, skip_weight)
    activity = hidden.astype(jnp.float32)
    channels, positions = activity.shape
    squares = lax.psum(jnp.sum(activity * activity, axis=0), "chan")
    mean_sq = squares / (channels * lax.axis_size("chan")) + epsilon
    normed = activity * lax.rsqrt(mean_sq)[None, :] * norm_gain[:, None]
    signal = gate_in.astype(jnp.float32) * normed
    groups = lax.axis_size("seq")
    width = positions // groups
    period = 2 * positions * groups
    conv = four_step(signal, filters, groups, width, period)
    mixed = gate_out.astype(jnp.float32) * (conv + skip_weight[:, None] * signal)
    return mixed.astype(jnp.bfloat16)


def solution(mesh):
    placed = (
        P("chan", "seq"),
        P("chan", "seq"),
        P("chan", "seq"),
        P("chan", "seq"),
        P("chan"),
        P("chan"),
    )
    return jax.shard_map(
        per_device, mesh=mesh, in_specs=placed, out_specs=P("chan", "seq"), check_vma=False
    )
```

```python
import functools
import math

import jax
import jax.numpy as jnp
import numpy as np
from jax import lax
from jax.experimental import pallas as pl
from jax.experimental.pallas import tpu as pltpu
from jax.sharding import PartitionSpec as P

highest = lax.Precision.HIGHEST
epsilon = 1e-06


def angle_table(row_count, col_count, period, sign):
    row_index = lax.iota(jnp.int32, row_count)[:, None]
    col_index = lax.iota(jnp.int32, col_count)[None, :]
    phase = (row_index * col_index % period).astype(jnp.float32) * (2.0 * math.pi / period)
    return (jnp.cos(phase), sign * jnp.sin(phase))


def twiddle_table(row_count, col_count, span, offset, period, sign):
    row_index = lax.iota(jnp.int32, row_count)[:, None]
    col_index = (lax.iota(jnp.int32, col_count) % span + offset)[None, :]
    phase = (row_index * col_index % period).astype(jnp.float32) * (2.0 * math.pi / period)
    return (jnp.cos(phase), sign * jnp.sin(phase))


def rotate(left_real, left_imag, right_real, right_imag):
    return (
        left_real * right_real - left_imag * right_imag,
        left_real * right_imag + left_imag * right_real,
    )


def sequence_forward(block, groups, span, offset, period):
    rows = 2 * groups
    cosine, sine = angle_table(rows, groups, rows, -1.0)
    both = jnp.dot(jnp.concatenate([cosine, sine], axis=0), block, precision=highest)
    real_part, imag_part = (both[:rows], both[rows:])
    turn_real, turn_imag = twiddle_table(rows, block.shape[1], span, offset, period, -1.0)
    return rotate(real_part, imag_part, turn_real, turn_imag)


def sequence_inverse(real_part, imag_part, groups, span, offset, period):
    rows = 2 * groups
    turn_real, turn_imag = twiddle_table(rows, real_part.shape[1], span, offset, period, 1.0)
    real_part, imag_part = rotate(real_part, imag_part, turn_real, turn_imag)
    cosine, sine = angle_table(groups, rows, rows, 1.0)
    return jnp.dot(cosine, real_part, precision=highest) - jnp.dot(
        sine, imag_part, precision=highest
    )


def full_transform(stacked, sign):
    length = stacked.shape[1]
    cosine, sine = angle_table(length, length, length, sign)
    return jnp.dot(stacked, jnp.concatenate([cosine, sine], axis=1), precision=highest)


def spectral_product(signal_real, signal_imag, filter_real, filter_imag):
    count, length = signal_real.shape
    stacked = jnp.concatenate([signal_real, signal_imag, filter_real, filter_imag], axis=0)
    spectra = full_transform(stacked, -1.0)
    s_real = spectra[:count, :length] - spectra[count : 2 * count, length:]
    s_imag = spectra[:count, length:] + spectra[count : 2 * count, :length]
    f_real = spectra[2 * count : 3 * count, :length] - spectra[3 * count :, length:]
    f_imag = spectra[2 * count : 3 * count, length:] + spectra[3 * count :, :length]
    product_real, product_imag = rotate(s_real, s_imag, f_real, f_imag)
    back = full_transform(jnp.concatenate([product_real, product_imag], axis=0), 1.0)
    return (
        back[:count, :length] - back[count:, length:],
        back[:count, length:] + back[count:, :length],
    )


def four_step(signal, filters, groups, width, period):
    channels, positions = signal.shape
    spread_signal, spread_filter = (
        lax.all_to_all(signal, "seq", split_axis=1, concat_axis=0, tiled=True),
        lax.all_to_all(filters, "seq", split_axis=1, concat_axis=0, tiled=True),
    )
    flat = (groups, channels * width)
    offset = lax.axis_index("seq") * width
    signal_real, signal_imag = sequence_forward(
        spread_signal.reshape(flat), groups, width, offset, period
    )
    filter_real, filter_imag = sequence_forward(
        spread_filter.reshape(flat), groups, width, offset, period
    )
    middle = (2 * groups, channels, width)
    signal_real, signal_imag, filter_real, filter_imag = (
        lax.all_to_all(signal_real.reshape(middle), "seq", split_axis=0, concat_axis=2, tiled=True),
        lax.all_to_all(signal_imag.reshape(middle), "seq", split_axis=0, concat_axis=2, tiled=True),
        lax.all_to_all(filter_real.reshape(middle), "seq", split_axis=0, concat_axis=2, tiled=True),
        lax.all_to_all(filter_imag.reshape(middle), "seq", split_axis=0, concat_axis=2, tiled=True),
    )
    rows = (2 * channels, positions)
    back_real, back_imag = spectral_product(
        signal_real.reshape(rows),
        signal_imag.reshape(rows),
        filter_real.reshape(rows),
        filter_imag.reshape(rows),
    )
    split = (2, channels, positions)
    back_real, back_imag = (
        lax.all_to_all(back_real.reshape(split), "seq", split_axis=2, concat_axis=0, tiled=True),
        lax.all_to_all(back_imag.reshape(split), "seq", split_axis=2, concat_axis=0, tiled=True),
    )
    wide = (2 * groups, channels * width)
    field = sequence_inverse(
        back_real.reshape(wide), back_imag.reshape(wide), groups, width, offset, period
    )
    result = lax.all_to_all(
        field.reshape(groups, channels, width), "seq", split_axis=0, concat_axis=2, tiled=True
    )
    return result.reshape(channels, positions) / period


def split_table(table):
    high = table.astype(jnp.bfloat16)
    low = (table - high.astype(np.float64)).astype(jnp.bfloat16)
    return high, low


def transform_tables(length, chunk, blocks):
    place = np.arange(length)[:, None]
    odd = 2 * np.arange(length)[None, :] + 1
    phase = (place * odd % (4 * length)) * (2.0 * np.pi / (4 * length))
    chunks = length // chunk
    cosine = np.cos(phase).reshape(length, chunks, chunk)
    sine = np.sin(phase).reshape(length, chunks, chunk)
    both = np.concatenate([cosine, -sine], axis=2)
    forward = both.transpose(1, 0, 2)
    inverse = both.reshape(length, 2 * length).T / length
    inverse = inverse.reshape(2 * length, blocks, length // blocks).transpose(1, 0, 2)
    return split_table(forward) + split_table(inverse)


def halves(value):
    high = value.astype(jnp.bfloat16)
    return high, (value - high.astype(jnp.float32)).astype(jnp.bfloat16)


def column(row, count, width):
    square = jnp.transpose(jnp.broadcast_to(row, (128, count)))
    return jnp.concatenate([square] * (width // 128), axis=1)


def conv_kernel(
    groups, peers, hidden_hbm, gate_hbm, filters, gain, skip, fwd_hi, fwd_lo, inv_hi, inv_lo,
    conv_in,
    fh, fl, ih, il, hidden, gate_in, filter_in, signal_in, conv_out, signal, local_sum, sums, halved_filter, halved, spectrum,
    product,
    table_sem, own_sem, f_send, f_recv, s_send, s_recv, c_send, c_recv, q_send, q_recv,
):
    me = lax.axis_index("seq")
    row = lax.axis_index("chan")
    count = hidden.shape[0] // groups
    width = hidden.shape[1]
    parts = signal_in.shape[0]
    sub = count // parts

    def local(source, target, sem):
        copy = pltpu.make_async_copy(source, target, sem)
        copy.start()
        return copy

    def send(slot, step, source, target, sent, received):
        copy = pltpu.make_async_remote_copy(
            src_ref=source, dst_ref=target, send_sem=sent.at[slot], recv_sem=received.at[slot],
            device_id={"seq": lax.rem(me + step, groups)}, device_id_type=pl.DeviceIdType.MESH,
        )
        copy.start()
        return copy

    barrier = pltpu.get_barrier_semaphore()
    for step in range(1, peers):
        pl.semaphore_signal(
            barrier, inc=1, device_id={"chan": lax.rem(row + step, peers)}, device_id_type=pl.DeviceIdType.MESH
        )
    for step in range(1, groups):
        pl.semaphore_signal(
            barrier, inc=1, device_id={"seq": lax.rem(me + step, groups)}, device_id_type=pl.DeviceIdType.MESH
        )
    own_hidden = local(hidden_hbm, hidden, own_sem.at[1])
    own_gate = local(gate_hbm, gate_in, own_sem.at[2])
    own_filter = local(
        filters.at[pl.ds(pl.multiple_of(me * count, count), count), :], filter_in.at[me], own_sem.at[0]
    )
    tables = [
        local(source, target, table_sem.at[index])
        for index, (source, target) in enumerate(((fwd_hi, fh), (fwd_lo, fl), (inv_hi, ih), (inv_lo, il)))
    ]
    pl.semaphore_wait(barrier, groups + peers - 2)

    order = [groups // 2] + [s for s in range(1, groups) if s != groups // 2]

    filter_copies = [
        send(
            step,
            step,
            filters.at[pl.ds(pl.multiple_of(lax.rem(me + step, groups) * count, count), count), :],
            filter_in.at[me],
            f_send,
            f_recv,
        )
        for step in range(1, groups)
    ]
    own_hidden.wait()
    partial = jnp.zeros((1, width), jnp.float32)
    for block in range(groups):
        activity = hidden[block * count : (block + 1) * count, :].astype(jnp.float32)
        partial = partial + jnp.sum(activity * activity, axis=0, keepdims=True)
    local_sum[...] = partial
    sums[row] = partial
    sum_copies = []
    for step in range(1, peers):
        copy = pltpu.make_async_remote_copy(
            src_ref=local_sum, dst_ref=sums.at[row], send_sem=q_send.at[step], recv_sem=q_recv.at[step],
            device_id={"chan": lax.rem(row + step, peers)}, device_id_type=pl.DeviceIdType.MESH,
        )
        copy.start()
        sum_copies.append(copy)
    own_gate.wait()
    for block in range(groups):
        gains = column(gain[block], count, width)
        for part in range(parts):
            rows = slice(block * count + part * sub, block * count + (part + 1) * sub)
            scaled = hidden[rows, :].astype(jnp.float32) * gains[part * sub : (part + 1) * sub]
            signal[part, block] = gate_in[rows, :].astype(jnp.float32) * scaled
    for copy in sum_copies:
        copy.wait()
    total = sums[0]
    for index in range(1, peers):
        total = total + sums[index]
    scale = lax.rsqrt(total / (hidden.shape[0] * peers) + epsilon)
    signal_copies = []
    for part in range(parts):
        copies = []
        for step in range(1, groups):
            to = lax.rem(me + step, groups)
            signal[part, to] = signal[part, to] * scale
            copies.append(
                send(part * groups + step, step, signal.at[part, to], signal_in.at[part, me], s_send, s_recv)
            )
        signal_in[part, me] = signal[part, me] * scale
        signal_copies.append(copies)

    chunks = fh.shape[0]
    chunk = fh.shape[2] // 2

    def store_halves(target, block, value):
        size = value.shape[0]
        high, low = halves(value)
        target[:size, block * width : (block + 1) * width] = high
        target[size:, block * width : (block + 1) * width] = low

    def transform(source, index):
        size = source.shape[0] // 2
        both = jnp.dot(source[...], fh[index], preferred_element_type=jnp.float32)
        small = jnp.dot(source[:size, :], fl[index], preferred_element_type=jnp.float32)
        return both[:size] + (both[size:] + small)

    def filter_step(index, carry):
        spectrum[index] = transform(halved_filter, index)
        return carry

    weights = column(skip[me], count, width)

    def invert(part, block):
        both = jnp.dot(product[...], ih[block], preferred_element_type=jnp.float32)
        small = jnp.dot(product[:sub, :], il[block], preferred_element_type=jnp.float32)
        conv = both[:sub] + (both[sub:] + small)
        return conv + weights[part * sub : (part + 1) * sub] * signal_in[part, block]

    own_filter.wait()
    for copy in filter_copies:
        copy.wait()
    for block in range(groups):
        store_halves(halved_filter, block, filter_in[block])
    tables[0].wait()
    tables[1].wait()
    lax.fori_loop(0, chunks, filter_step, 0)
    conv_copies = []
    for part in range(parts):
        for copy in signal_copies[part]:
            copy.wait()
        for block in range(groups):
            store_halves(halved, block, signal_in[part, block])
        for index in range(chunks):
            s_both = transform(halved, index)
            s_real, s_imag = s_both[:, :chunk], s_both[:, chunk:]
            f_both = spectrum[index][part * sub : (part + 1) * sub]
            f_real, f_imag = f_both[:, :chunk], f_both[:, chunk:]
            real_high, real_low = halves(s_real * f_real - s_imag * f_imag)
            imag_high, imag_low = halves(s_real * f_imag + s_imag * f_real)
            start = 2 * index * chunk
            product[:sub, start : start + chunk] = real_high
            product[sub:, start : start + chunk] = real_low
            product[:sub, start + chunk : start + 2 * chunk] = imag_high
            product[sub:, start + chunk : start + 2 * chunk] = imag_low
        if part == 0:
            tables[2].wait()
            tables[3].wait()
        for step in order:
            to = lax.rem(me + step, groups)
            conv_out[part, to] = invert(part, to)
            conv_copies.append(
                send(part * groups + step, step, conv_out.at[part, to], conv_in.at[me, part], c_send, c_recv)
            )
        conv_out[part, me] = invert(part, me)
        conv_copies.append(local(conv_out.at[part, me], conv_in.at[me, part], own_sem.at[3 + part]))
    for copy in conv_copies:
        copy.wait()


def fused(hidden, gate_in, gate_out, filters, norm_gain, skip_weight):
    channels, width = hidden.shape
    groups, peers = lax.axis_size("seq"), lax.axis_size("chan")
    length, count = groups * width, channels // groups
    chunk = min(256, length)
    tables = [jnp.asarray(t) for t in transform_tables(length, chunk, groups)]
    vmem = pl.BlockSpec(memory_space=pltpu.VMEM)
    hbm = pl.BlockSpec(memory_space=pl.ANY)
    parts = 2
    sub = count // parts
    block = (parts, groups, sub, width)
    f32, bf16 = jnp.float32, jnp.bfloat16
    pair = pltpu.SemaphoreType.DMA((parts * groups,))
    ring = pltpu.SemaphoreType.DMA((peers,))
    conv = pl.pallas_call(
        functools.partial(conv_kernel, groups, peers),
        out_shape=jax.ShapeDtypeStruct((groups, parts, sub, width), f32),
        in_specs=[hbm, hbm, hbm, vmem, vmem, hbm, hbm, hbm, hbm],
        out_specs=hbm,
        scratch_shapes=[
            pltpu.VMEM(tables[0].shape, bf16),
            pltpu.VMEM(tables[1].shape, bf16),
            pltpu.VMEM(tables[2].shape, bf16),
            pltpu.VMEM(tables[3].shape, bf16),
            pltpu.VMEM((channels, width), bf16),
            pltpu.VMEM((channels, width), bf16),
            pltpu.VMEM((groups, count, width), f32),
            pltpu.VMEM(block, f32),
            pltpu.VMEM(block, f32),
            pltpu.VMEM(block, f32),
            pltpu.VMEM((1, width), f32),
            pltpu.VMEM((peers, 1, width), f32),
            pltpu.VMEM((2 * count, length), bf16),
            pltpu.VMEM((2 * sub, length), bf16),
            pltpu.VMEM((length // chunk, count, 2 * chunk), f32),
            pltpu.VMEM((2 * sub, 2 * length), bf16),
            pltpu.SemaphoreType.DMA((4,)),
            pltpu.SemaphoreType.DMA((3 + parts,)),
            pair, pair, pair, pair, pair, pair, ring, ring,
        ],
        compiler_params=pltpu.CompilerParams(
            collective_id=0, has_side_effects=True, vmem_limit_bytes=56 * 1024 * 1024
        ),
    )(
        hidden, gate_in, filters,
        norm_gain.reshape(groups, 1, count), skip_weight.reshape(groups, 1, count), *tables,
    )
    mixed = gate_out.astype(f32) * conv.reshape(channels, width)
    return mixed.astype(bf16)


def per_device(hidden, gate_in, gate_out, filters, norm_gain, skip_weight):
    length = hidden.shape[1] * lax.axis_size("seq")
    if 16 * length * length <= 2**24 and hidden.shape[0] == 128 * lax.axis_size("seq"):
        return fused(hidden, gate_in, gate_out, filters, norm_gain, skip_weight)
    activity = hidden.astype(jnp.float32)
    channels, positions = activity.shape
    squares = lax.psum(jnp.sum(activity * activity, axis=0), "chan")
    mean_sq = squares / (channels * lax.axis_size("chan")) + epsilon
    normed = activity * lax.rsqrt(mean_sq)[None, :] * norm_gain[:, None]
    signal = gate_in.astype(jnp.float32) * normed
    groups = lax.axis_size("seq")
    width = positions // groups
    period = 2 * positions * groups
    conv = four_step(signal, filters, groups, width, period)
    mixed = gate_out.astype(jnp.float32) * (conv + skip_weight[:, None] * signal)
    return mixed.astype(jnp.bfloat16)


def solution(mesh):
    placed = (
        P("chan", "seq"),
        P("chan", "seq"),
        P("chan", "seq"),
        P("chan", "seq"),
        P("chan"),
        P("chan"),
    )
    return jax.shard_map(
        per_device, mesh=mesh, in_specs=placed, out_specs=P("chan", "seq"), check_vma=False
    )
```
